512 devices in a mesh: ctx: 32 (over z_hi, y), head: 16 (over x, z_lo, core).
Axes of the slice: x: 4, y: 8, z: 8 (z_hi: 4, z_lo: 2; z = z_hi * 2 + z_lo), core: 2. Of those that a mesh axis runs over, the one named last changes fastest.
Arguments:
- queries: bfloat16 [5120, 8192], P('ctx', 'head'), may hold values from -6 to 6
- keys: bfloat16 [5120, 2048], P('ctx', 'head'), may hold values from -6 to 6
- values: bfloat16 [5120, 2048], P('ctx', 'head'), may hold values from -6 to 6
- out_grad: bfloat16 [5120, 8192], P('ctx', 'head'), may hold values from -6 to 6
- order: int32 [64], replicated, may hold values from 0 to 63, as said below
Outputs:
- attention: bfloat16 [5120, 8192], P('ctx', 'head')
- grad_queries: bfloat16 [5120, 8192], P('ctx', 'head')
- grad_keys: bfloat16 [5120, 2048], P('ctx', 'head')
- grad_values: bfloat16 [5120, 2048], P('ctx', 'head')
The draws below stay inside these ranges and needn't reach their ends.
Inputs may be any that keep to these rules, and one draw needn't show every extreme that they name: order is a permutation of the 64 spans; row blocks 2i and 2i + 1 (the rows of index i of ctx) hold spans c and 63 - c for some c, in either order.
All inputs are finite; a program needn't handle non-finite values.
Results may differ from the reference program's by a relative error of at most 0.03.
Values may be sent and summed in bfloat16 or wider, within the bound.
No kernel may reach another device: no remote copies, remote signals or barrier semaphores. Data moves between devices by JAX's collectives and lax.ppermute only.
A program may use at most 64 MiB of HBM per device.

```python
import jax
import jax.numpy as jnp
from jax import lax

HEADS = 32
KV_HEADS = 8
HEAD_DIM = 128
BATCH = 2
SPAN = 80
NCHUNK = 64
SEQ = 5120
N_CTX = 32


def fold_order(key):
    base_key = jax.random.fold_in(key, 7)
    perm_key, flip_key = jax.random.split(base_key)
    chosen = jax.random.permutation(perm_key, N_CTX).astype(jnp.int32)
    flipped = jax.random.randint(flip_key, (N_CTX,), 0, 2, dtype=jnp.int32)
    lowhigh = jnp.stack([chosen, NCHUNK - 1 - chosen], axis=1)
    swapped = jnp.stack([lowhigh[:, 1], lowhigh[:, 0]], axis=1)
    return jnp.where(flipped[:, None] == 1, swapped, lowhigh).reshape(-1).astype(jnp.int32)


def draw_order(key, part):
    return fold_order(key)


def draw_queries(key, part):
    base_key = jax.random.fold_in(key, 21)
    drawn = jnp.clip(jax.random.normal(base_key, (SEQ, BATCH * HEADS * HEAD_DIM), jnp.float32), -6.0, 6.0)
    return drawn.astype(jnp.bfloat16)


def draw_keys(key, part):
    base_key = jax.random.fold_in(key, 22)
    drawn = jnp.clip(jax.random.normal(base_key, (SEQ, BATCH * KV_HEADS * HEAD_DIM), jnp.float32), -6.0, 6.0)
    return drawn.astype(jnp.bfloat16)


def block_scale(rng, dims, cuts, low, largest):
    def one(position, blocks):
        draws = jax.random.uniform(jax.random.fold_in(jax.random.fold_in(rng, 6), position), (blocks,), jnp.float32, low / len(cuts), largest / len(cuts))
        return jnp.repeat(jnp.exp(draws), dims[position] // blocks).reshape((-1,) + (1,) * (len(dims) - position - 1))

    loudness = one(*cuts[0])
    for cut in cuts[1:]:
        loudness = loudness * one(*cut)
    return loudness


def noise(own_key, extent, spread, most, pieces=(), held_as=jnp.bfloat16):
    result = spread * jax.random.normal(own_key, extent, jnp.float32)
    if pieces:
        result = result * block_scale(own_key, extent, pieces, -0.22, 0.18)
    return jnp.clip(result, -most, most).astype(held_as)


def setup_inputs(seed: int = 0) -> dict:
    arg_keys = jax.random.split(jax.random.key(seed), 6)
    queries = draw_queries(jax.random.fold_in(arg_keys[5], 71), 0)
    keys = draw_keys(jax.random.fold_in(arg_keys[5], 71), 0)
    values = noise(arg_keys[2], (SEQ, BATCH * KV_HEADS * HEAD_DIM), 1.0, 6.0, ((0, 32), (1, 16)))
    out_grad = noise(arg_keys[3], (SEQ, BATCH * HEADS * HEAD_DIM), 1.0, 6.0, ((0, 32), (1, 16)))
    order = draw_order(jax.random.fold_in(arg_keys[5], 71), 0)
    return {"queries": queries, "keys": keys, "values": values, "out_grad": out_grad, "order": order}


NEG = -1e30


def reference(queries, keys, values, out_grad, order):
    seq_len = queries.shape[0]
    score_scale = 1.0 / (HEAD_DIM ** 0.5)
    group_size = HEADS // KV_HEADS
    all_heads = BATCH * HEADS
    all_kv = BATCH * KV_HEADS
    row_ids = jnp.arange(seq_len, dtype=jnp.int32)
    positions = order[row_ids // SPAN] * SPAN + row_ids % SPAN
    visible = positions[None, :] <= positions[:, None]
    blocked_visible = visible.reshape(seq_len, NCHUNK, SPAN)

    def split_heads(array, head_count):
        return array.reshape(seq_len, head_count, HEAD_DIM).transpose(1, 0, 2)

    query_heads = split_heads(queries, all_heads)
    grad_heads = split_heads(out_grad, all_heads)
    key_heads = jnp.repeat(split_heads(keys, all_kv), group_size, axis=0)
    value_heads = jnp.repeat(split_heads(values, all_kv), group_size, axis=0)

    def one_head(inputs):
        query_h, key_h, value_h, grad_h = inputs
        scores = jnp.dot(query_h, key_h.T, preferred_element_type=jnp.float32) * score_scale
        scores = jnp.where(visible, scores, NEG)
        blocked = scores.reshape(seq_len, NCHUNK, SPAN)
        block_max = jnp.max(blocked, axis=2)
        block_weights = jnp.where(blocked_visible, jnp.exp(blocked - block_max[:, :, None]), 0.0)
        block_total = jnp.sum(block_weights, axis=2)
        weights_low = lax.optimization_barrier(block_weights.astype(jnp.bfloat16)).astype(jnp.float32)
        row_max = jnp.max(block_max, axis=1)
        block_factor = jnp.exp(block_max - row_max[:, None])
        row_total = jnp.sum(block_factor * block_total, axis=1)
        scaled_weights = (block_factor[:, :, None] * weights_low).reshape(seq_len, seq_len)
        attention = jnp.dot(scaled_weights, value_h.astype(jnp.float32), precision=lax.Precision.HIGHEST)
        attention = (attention / row_total[:, None]).astype(jnp.bfloat16)
        log_total = row_max + jnp.log(row_total)
        row_dot = jnp.sum(grad_h.astype(jnp.float32) * attention.astype(jnp.float32), axis=1)
        probs = jnp.where(visible, jnp.exp(scores - log_total[:, None]), 0.0)
        probs_low = probs.astype(jnp.bfloat16)
        grad_value = jnp.dot(probs_low.T, grad_h, preferred_element_type=jnp.float32)
        grad_probs = jnp.dot(grad_h, value_h.T, preferred_element_type=jnp.float32)
        grad_scores = (probs * (grad_probs - row_dot[:, None])).astype(jnp.bfloat16)
        grad_query = jnp.dot(grad_scores, key_h, preferred_element_type=jnp.float32)
        grad_key = jnp.dot(grad_scores.T, query_h, preferred_element_type=jnp.float32)
        return attention, grad_query, grad_key, grad_value

    attention, grad_query, grad_key, grad_value = lax.map(one_head, (query_heads, key_heads, value_heads, grad_heads))

    def join_heads(array):
        return array.transpose(1, 0, 2).reshape(seq_len, -1)

    grad_key = jnp.sum(grad_key.reshape(all_kv, group_size, seq_len, HEAD_DIM), axis=1)
    grad_value = jnp.sum(grad_value.reshape(all_kv, group_size, seq_len, HEAD_DIM), axis=1)
    grad_queries = join_heads((score_scale * grad_query).astype(jnp.bfloat16))
    grad_keys = join_heads((score_scale * grad_key).astype(jnp.bfloat16))
    grad_values = join_heads(grad_value.astype(jnp.bfloat16))
    return (join_heads(attention), grad_queries, grad_keys, grad_values)
```

```python
import math

import jax
import jax.numpy as jnp
from jax import lax
from jax.experimental import pallas as pl
from jax.experimental.pallas import tpu as pltpu
from jax.sharding import PartitionSpec as P

HEADS = 32
KV_HEADS = 8
HEAD_DIM = 128
SPAN = 80
KEY_BLOCK = 512

NEG = -1e30


def attention_kernel(
    limits_ref, q_ref, g_ref, kv_ref, qpos_ref,
    out_ref, dq_ref, dkv_ref,
    top_ref, total_ref, acc_ref, lse_ref, dot_ref, dqacc_ref,
):
    rows = q_ref.shape[0]
    half = rows // 2
    width = HEAD_DIM
    scale = 1.0 / math.sqrt(width)
    early_blocks = limits_ref[0]
    late_blocks = limits_ref[1]

    top_ref[...] = jnp.full(top_ref.shape, NEG, jnp.float32)
    total_ref[...] = jnp.zeros(total_ref.shape, jnp.float32)
    acc_ref[...] = jnp.zeros(acc_ref.shape, jnp.float32)

    def scores_of(lo, count, start):
        q = q_ref[lo:lo + count, :]
        k = kv_ref[pl.ds(start, KEY_BLOCK), 0:width]
        s = lax.dot_general(q, k, (((1,), (1,)), ((), ())), preferred_element_type=jnp.float32) * scale
        kpos = start + lax.broadcasted_iota(jnp.int32, (1, KEY_BLOCK), 1)
        visible = kpos <= qpos_ref[lo:lo + count, :]
        return s, visible

    def forward_block(lo, count, block):
        start = pl.multiple_of(block * KEY_BLOCK, KEY_BLOCK)
        s, visible = scores_of(lo, count, start)
        s = jnp.where(visible, s, NEG)
        old_top = top_ref[lo:lo + count, :]
        new_top = jnp.maximum(old_top, jnp.max(s, axis=1, keepdims=True))
        p = jnp.where(visible, jnp.exp(s - new_top), 0.0)
        rescale = jnp.exp(old_top - new_top)
        total_ref[lo:lo + count, :] = total_ref[lo:lo + count, :] * rescale + jnp.sum(p, axis=1, keepdims=True)
        v = kv_ref[pl.ds(start, KEY_BLOCK), width:2 * width]
        pv = jnp.dot(p.astype(jnp.bfloat16), v, preferred_element_type=jnp.float32)
        acc_ref[lo:lo + count, :] = acc_ref[lo:lo + count, :] * rescale + pv
        top_ref[lo:lo + count, :] = new_top

    def fwd_both(block, carry):
        forward_block(0, rows, block)
        return carry

    def fwd_late(block, carry):
        forward_block(half, half, block)
        return carry

    lax.fori_loop(0, early_blocks, fwd_both, 0)
    lax.fori_loop(early_blocks, late_blocks, fwd_late, 0)

    attention = (acc_ref[...] / total_ref[...]).astype(jnp.bfloat16)
    out_ref[...] = attention
    lse_ref[...] = top_ref[...] + jnp.log(total_ref[...])
    dot_ref[...] = jnp.sum(
        g_ref[...].astype(jnp.float32) * attention.astype(jnp.float32), axis=1, keepdims=True
    )
    dqacc_ref[...] = jnp.zeros(dqacc_ref.shape, jnp.float32)
    dkv_ref[...] = jnp.zeros(dkv_ref.shape, jnp.float32)

    def backward_block(lo, count, block):
        start = pl.multiple_of(block * KEY_BLOCK, KEY_BLOCK)
        s, visible = scores_of(lo, count, start)
        probs = jnp.where(visible, jnp.exp(s - lse_ref[lo:lo + count, :]), 0.0)
        g = g_ref[lo:lo + count, :]
        k = kv_ref[pl.ds(start, KEY_BLOCK), 0:width]
        v = kv_ref[pl.ds(start, KEY_BLOCK), width:2 * width]
        grad_probs = lax.dot_general(g, v, (((1,), (1,)), ((), ())), preferred_element_type=jnp.float32)
        grad_scores = (probs * (grad_probs - dot_ref[lo:lo + count, :])).astype(jnp.bfloat16)
        dqacc_ref[lo:lo + count, :] += jnp.dot(grad_scores, k, preferred_element_type=jnp.float32)
        q = q_ref[lo:lo + count, :]
        dk = lax.dot_general(grad_scores, q, (((0,), (0,)), ((), ())), preferred_element_type=jnp.float32)
        dv = lax.dot_general(
            probs.astype(jnp.bfloat16), g, (((0,), (0,)), ((), ())), preferred_element_type=jnp.float32
        )
        dkv_ref[pl.ds(start, KEY_BLOCK), 0:width] += dk
        dkv_ref[pl.ds(start, KEY_BLOCK), width:2 * width] += dv

    def bwd_both(block, carry):
        backward_block(0, rows, block)
        return carry

    def bwd_late(block, carry):
        backward_block(half, half, block)
        return carry

    lax.fori_loop(0, early_blocks, bwd_both, 0)
    lax.fori_loop(early_blocks, late_blocks, bwd_late, 0)
    dq_ref[...] = (dqacc_ref[...] * scale).astype(jnp.bfloat16)


def local_attention(limits, q_rows, g_rows, kv_sorted, q_pos):
    rows, width = q_rows.shape
    keys = kv_sorted.shape[0]
    vmem = pltpu.VMEM
    flops = 2 * rows * keys * width * 7 // 2
    return pl.pallas_call(
        attention_kernel,
        out_shape=(
            jax.ShapeDtypeStruct((rows, width), jnp.bfloat16),
            jax.ShapeDtypeStruct((rows, width), jnp.bfloat16),
            jax.ShapeDtypeStruct((keys, 2 * width), jnp.float32),
        ),
        in_specs=[
            pl.BlockSpec(memory_space=pltpu.SMEM),
            pl.BlockSpec(memory_space=vmem),
            pl.BlockSpec(memory_space=vmem),
            pl.BlockSpec(memory_space=vmem),
            pl.BlockSpec(memory_space=vmem),
        ],
        out_specs=(
            pl.BlockSpec(memory_space=vmem),
            pl.BlockSpec(memory_space=vmem),
            pl.BlockSpec(memory_space=vmem),
        ),
        scratch_shapes=[
            pltpu.VMEM((rows, 1), jnp.float32),
            pltpu.VMEM((rows, 1), jnp.float32),
            pltpu.VMEM((rows, width), jnp.float32),
            pltpu.VMEM((rows, 1), jnp.float32),
            pltpu.VMEM((rows, 1), jnp.float32),
            pltpu.VMEM((rows, width), jnp.float32),
        ],
        cost_estimate=pl.CostEstimate(
            flops=flops, transcendentals=rows * keys, bytes_accessed=keys * width * 12
        ),
    )(limits, q_rows, g_rows, kv_sorted, q_pos)


def on_device(queries, keys, values, out_grad, order):
    row_count = queries.shape[0]
    width = HEAD_DIM
    score_scale = 1.0 / math.sqrt(width)
    cycle_size = lax.axis_size("ctx")
    span_count = 2 * cycle_size
    my_index = lax.axis_index("ctx")
    q_heads = queries.shape[1] // width

    kv_local = jnp.concatenate([keys, values], axis=1)
    kv_all = lax.all_gather(kv_local, "ctx", axis=0, tiled=True)
    inverse = jnp.zeros((span_count,), jnp.int32).at[order].set(jnp.arange(span_count, dtype=jnp.int32))
    kv_sorted = kv_all.reshape(span_count, SPAN, 2 * width)[inverse].reshape(span_count * SPAN, 2 * width)

    pair = lax.dynamic_slice_in_dim(order, 2 * my_index, 2)
    low_first = pair[0] < pair[1]
    my_low = jnp.minimum(pair[0], pair[1])
    early_keys = (my_low + 1) * SPAN
    late_keys = (span_count - my_low) * SPAN
    limits = jnp.stack(
        [(early_keys + KEY_BLOCK - 1) // KEY_BLOCK, (late_keys + KEY_BLOCK - 1) // KEY_BLOCK]
    ).astype(jnp.int32)

    def to_rows(array):
        blocks = array.reshape(2, SPAN, q_heads, width)
        blocks = jnp.where(low_first, blocks, blocks[::-1])
        return blocks.transpose(0, 2, 1, 3).reshape(2 * q_heads * SPAN, width)

    def from_rows(array):
        blocks = array.reshape(2, q_heads, SPAN, width).transpose(0, 2, 1, 3)
        blocks = jnp.where(low_first, blocks, blocks[::-1])
        return blocks.reshape(row_count, q_heads * width)

    offsets = jnp.arange(SPAN, dtype=jnp.int32)
    span_pos = jnp.stack([my_low, span_count - 1 - my_low])[:, None] * SPAN + offsets[None, :]
    q_pos = jnp.broadcast_to(span_pos[:, None, :], (2, q_heads, SPAN)).reshape(-1, 1)

    attention_rows, dq_rows, dkv_sorted = local_attention(
        limits, to_rows(queries), to_rows(out_grad), kv_sorted, q_pos
    )
    dkv_all = dkv_sorted.reshape(span_count, SPAN, 2 * width)[order].reshape(-1, 2 * width)
    dkv_mine = lax.psum_scatter(dkv_all, "ctx", scatter_dimension=0, tiled=True)
    grad_keys = (score_scale * dkv_mine[:, :width]).astype(jnp.bfloat16)
    grad_values = dkv_mine[:, width:].astype(jnp.bfloat16)
    return (from_rows(attention_rows), from_rows(dq_rows), grad_keys, grad_values)


def solution(mesh):
    return jax.shard_map(
        on_device,
        mesh=mesh,
        in_specs=(P("ctx", "head"), P("ctx", "head"), P("ctx", "head"), P("ctx", "head"), P()),
        out_specs=(P("ctx", "head"), P("ctx", "head"), P("ctx", "head"), P("ctx", "head")),
        check_vma=False,
    )
```

```python
import math

import jax
import jax.numpy as jnp
from jax import lax
from jax.experimental import pallas as pl
from jax.experimental.pallas import tpu as pltpu
from jax.sharding import Mesh
from jax.sharding import PartitionSpec as P

HEADS = 32
KV_HEADS = 8
HEAD_DIM = 128
SPAN = 80
KEY_BLOCK = 512

NEG = -1e30
CTX = ("zh", "y")


def attention_kernel(
    limits_ref, q_ref, g_ref, kv_ref, qpos_ref,
    out_ref, dq_ref, dkv_ref,
    top_ref, total_ref, acc_ref, lse_ref, dot_ref, dqacc_ref,
):
    rows = q_ref.shape[0]
    half = rows // 2
    width = HEAD_DIM
    scale = 1.0 / math.sqrt(width)
    early_blocks = limits_ref[0]
    late_blocks = limits_ref[1]

    top_ref[...] = jnp.full(top_ref.shape, NEG, jnp.float32)
    total_ref[...] = jnp.zeros(total_ref.shape, jnp.float32)
    acc_ref[...] = jnp.zeros(acc_ref.shape, jnp.float32)

    def scores_of(lo, count, start):
        q = q_ref[lo:lo + count, :]
        k = kv_ref[pl.ds(start, KEY_BLOCK), 0:width]
        s = lax.dot_general(q, k, (((1,), (1,)), ((), ())), preferred_element_type=jnp.float32) * scale
        kpos = start + lax.broadcasted_iota(jnp.int32, (1, KEY_BLOCK), 1)
        visible = kpos <= qpos_ref[lo:lo + count, :]
        return s, visible

    def forward_block(lo, count, block):
        start = pl.multiple_of(block * KEY_BLOCK, KEY_BLOCK)
        s, visible = scores_of(lo, count, start)
        s = jnp.where(visible, s, NEG)
        old_top = top_ref[lo:lo + count, :]
        new_top = jnp.maximum(old_top, jnp.max(s, axis=1, keepdims=True))
        p = jnp.where(visible, jnp.exp(s - new_top), 0.0)
        rescale = jnp.exp(old_top - new_top)
        total_ref[lo:lo + count, :] = total_ref[lo:lo + count, :] * rescale + jnp.sum(p, axis=1, keepdims=True)
        v = kv_ref[pl.ds(start, KEY_BLOCK), width:2 * width]
        pv = jnp.dot(p.astype(jnp.bfloat16), v, preferred_element_type=jnp.float32)
        acc_ref[lo:lo + count, :] = acc_ref[lo:lo + count, :] * rescale + pv
        top_ref[lo:lo + count, :] = new_top

    def fwd_both(block, carry):
        forward_block(0, rows, block)
        return carry

    def fwd_late(block, carry):
        forward_block(half, half, block)
        return carry

    lax.fori_loop(0, early_blocks, fwd_both, 0)
    lax.fori_loop(early_blocks, late_blocks, fwd_late, 0)

    attention = (acc_ref[...] / total_ref[...]).astype(jnp.bfloat16)
    out_ref[...] = attention
    lse_ref[...] = top_ref[...] + jnp.log(total_ref[...])
    dot_ref[...] = jnp.sum(
        g_ref[...].astype(jnp.float32) * attention.astype(jnp.float32), axis=1, keepdims=True
    )
    dqacc_ref[...] = jnp.zeros(dqacc_ref.shape, jnp.float32)
    dkv_ref[...] = jnp.zeros(dkv_ref.shape, jnp.float32)

    def backward_block(lo, count, block):
        start = pl.multiple_of(block * KEY_BLOCK, KEY_BLOCK)
        s, visible = scores_of(lo, count, start)
        probs = jnp.where(visible, jnp.exp(s - lse_ref[lo:lo + count, :]), 0.0)
        g = g_ref[lo:lo + count, :]
        k = kv_ref[pl.ds(start, KEY_BLOCK), 0:width]
        v = kv_ref[pl.ds(start, KEY_BLOCK), width:2 * width]
        grad_probs = lax.dot_general(g, v, (((1,), (1,)), ((), ())), preferred_element_type=jnp.float32)
        grad_scores = (probs * (grad_probs - dot_ref[lo:lo + count, :])).astype(jnp.bfloat16)
        dqacc_ref[lo:lo + count, :] += jnp.dot(grad_scores, k, preferred_element_type=jnp.float32)
        q = q_ref[lo:lo + count, :]
        dk = lax.dot_general(grad_scores, q, (((0,), (0,)), ((), ())), preferred_element_type=jnp.float32)
        dv = lax.dot_general(
            probs.astype(jnp.bfloat16), g, (((0,), (0,)), ((), ())), preferred_element_type=jnp.float32
        )
        dkv_ref[pl.ds(start, KEY_BLOCK), 0:width] += dk
        dkv_ref[pl.ds(start, KEY_BLOCK), width:2 * width] += dv

    def bwd_both(block, carry):
        backward_block(0, rows, block)
        return carry

    def bwd_late(block, carry):
        backward_block(half, half, block)
        return carry

    lax.fori_loop(0, early_blocks, bwd_both, 0)
    lax.fori_loop(early_blocks, late_blocks, bwd_late, 0)
    dq_ref[...] = (dqacc_ref[...] * scale).astype(jnp.bfloat16)


def local_attention(limits, q_rows, g_rows, kv_sorted, q_pos):
    rows, width = q_rows.shape
    keys = kv_sorted.shape[0]
    vmem = pltpu.VMEM
    flops = 2 * rows * keys * width * 7 // 2
    return pl.pallas_call(
        attention_kernel,
        out_shape=(
            jax.ShapeDtypeStruct((rows, width), jnp.bfloat16),
            jax.ShapeDtypeStruct((rows, width), jnp.bfloat16),
            jax.ShapeDtypeStruct((keys, 2 * width), jnp.float32),
        ),
        in_specs=[
            pl.BlockSpec(memory_space=pltpu.SMEM),
            pl.BlockSpec(memory_space=vmem),
            pl.BlockSpec(memory_space=vmem),
            pl.BlockSpec(memory_space=vmem),
            pl.BlockSpec(memory_space=vmem),
        ],
        out_specs=(
            pl.BlockSpec(memory_space=vmem),
            pl.BlockSpec(memory_space=vmem),
            pl.BlockSpec(memory_space=vmem),
        ),
        scratch_shapes=[
            pltpu.VMEM((rows, 1), jnp.float32),
            pltpu.VMEM((rows, 1), jnp.float32),
            pltpu.VMEM((rows, width), jnp.float32),
            pltpu.VMEM((rows, 1), jnp.float32),
            pltpu.VMEM((rows, 1), jnp.float32),
            pltpu.VMEM((rows, width), jnp.float32),
        ],
        cost_estimate=pl.CostEstimate(
            flops=flops, transcendentals=rows * keys, bytes_accessed=keys * width * 12
        ),
    )(limits, q_rows, g_rows, kv_sorted, q_pos)


def on_device(queries, keys, values, out_grad, order):
    row_count = queries.shape[0]
    width = HEAD_DIM
    score_scale = 1.0 / math.sqrt(width)
    cycle_size = lax.axis_size(CTX)
    span_count = 2 * cycle_size
    my_index = lax.axis_index(CTX)
    q_heads = queries.shape[1] // width

    outer = lax.axis_size("zh")
    inner = lax.axis_size("y")
    kv_local = jnp.concatenate([keys, values], axis=1)
    kv_all = lax.all_gather(lax.all_gather(kv_local, "zh", axis=0, tiled=True), "y", axis=0, tiled=True)
    kv_all = kv_all.reshape(inner, outer, 2 * SPAN, 2 * width).transpose(1, 0, 2, 3)
    inverse = jnp.zeros((span_count,), jnp.int32).at[order].set(jnp.arange(span_count, dtype=jnp.int32))
    kv_sorted = kv_all.reshape(span_count, SPAN, 2 * width)[inverse].reshape(span_count * SPAN, 2 * width)

    pair = lax.dynamic_slice_in_dim(order, 2 * my_index, 2)
    low_first = pair[0] < pair[1]
    my_low = jnp.minimum(pair[0], pair[1])
    early_keys = (my_low + 1) * SPAN
    late_keys = (span_count - my_low) * SPAN
    limits = jnp.stack(
        [(early_keys + KEY_BLOCK - 1) // KEY_BLOCK, (late_keys + KEY_BLOCK - 1) // KEY_BLOCK]
    ).astype(jnp.int32)

    def to_rows(array):
        blocks = array.reshape(2, SPAN, q_heads, width)
        blocks = jnp.where(low_first, blocks, blocks[::-1])
        return blocks.transpose(0, 2, 1, 3).reshape(2 * q_heads * SPAN, width)

    def from_rows(array):
        blocks = array.reshape(2, q_heads, SPAN, width).transpose(0, 2, 1, 3)
        blocks = jnp.where(low_first, blocks, blocks[::-1])
        return blocks.reshape(row_count, q_heads * width)

    offsets = jnp.arange(SPAN, dtype=jnp.int32)
    span_pos = jnp.stack([my_low, span_count - 1 - my_low])[:, None] * SPAN + offsets[None, :]
    q_pos = jnp.broadcast_to(span_pos[:, None, :], (2, q_heads, SPAN)).reshape(-1, 1)

    attention_rows, dq_rows, dkv_sorted = local_attention(
        limits, to_rows(queries), to_rows(out_grad), kv_sorted, q_pos
    )
    dkv_all = dkv_sorted.reshape(span_count, SPAN, 2 * width)[order].reshape(cycle_size, 2 * SPAN, 2 * width)
    dkv_parts = lax.all_to_all(dkv_all.astype(jnp.bfloat16), CTX, 0, 0, tiled=False)
    dkv_mine = jnp.sum(dkv_parts.astype(jnp.float32), axis=0)
    grad_keys = (score_scale * dkv_mine[:, :width]).astype(jnp.bfloat16)
    grad_values = dkv_mine[:, width:].astype(jnp.bfloat16)
    return (from_rows(attention_rows), from_rows(dq_rows), grad_keys, grad_values)


def solution(mesh):
    ctx_size = mesh.shape["ctx"]
    outer = 4 if ctx_size % 4 == 0 else 1
    split = Mesh(
        mesh.devices.reshape(outer, ctx_size // outer, mesh.shape["head"]), ("zh", "y", "head")
    )
    rows = P(CTX, "head")
    return jax.shard_map(
        on_device,
        mesh=split,
        in_specs=(rows, rows, rows, rows, P()),
        out_specs=(rows, rows, rows, rows),
        check_vma=False,
    )
```

```python
import math

import jax
import jax.numpy as jnp
from jax import lax
from jax.experimental import pallas as pl
from jax.experimental.pallas import tpu as pltpu
from jax.sharding import Mesh
from jax.sharding import PartitionSpec as P

HEADS = 32
KV_HEADS = 8
HEAD_DIM = 128
SPAN = 80
KEY_BLOCK = 512

NEG = -1e30
CTX = ("zh", "y")


def attention_kernel(
    limits_ref, q_ref, g_ref, kv_ref, qpos_ref,
    out_ref, dq_ref, dkv_ref,
    top_ref, total_ref, acc_ref, lse_ref, dot_ref, dqacc_ref,
):
    rows = q_ref.shape[0]
    half = rows // 2
    width = HEAD_DIM
    scale = 1.0 / math.sqrt(width)
    early_blocks = limits_ref[0]
    late_blocks = limits_ref[1]

    top_ref[...] = jnp.full(top_ref.shape, NEG, jnp.float32)
    total_ref[...] = jnp.zeros(total_ref.shape, jnp.float32)
    acc_ref[...] = jnp.zeros(acc_ref.shape, jnp.float32)

    def scores_of(lo, count, start):
        q = q_ref[lo:lo + count, :]
        k = kv_ref[pl.ds(start, KEY_BLOCK), 0:width]
        s = lax.dot_general(q, k, (((1,), (1,)), ((), ())), preferred_element_type=jnp.float32) * scale
        kpos = start + lax.broadcasted_iota(jnp.int32, (1, KEY_BLOCK), 1)
        visible = kpos <= qpos_ref[lo:lo + count, :]
        return s, visible

    def forward_block(lo, count, block):
        start = pl.multiple_of(block * KEY_BLOCK, KEY_BLOCK)
        s, visible = scores_of(lo, count, start)
        s = jnp.where(visible, s, NEG)
        old_top = top_ref[lo:lo + count, :]
        new_top = jnp.maximum(old_top, jnp.max(s, axis=1, keepdims=True))
        p = jnp.where(visible, jnp.exp(s - new_top), 0.0)
        rescale = jnp.exp(old_top - new_top)
        total_ref[lo:lo + count, :] = total_ref[lo:lo + count, :] * rescale + jnp.sum(p, axis=1, keepdims=True)
        v = kv_ref[pl.ds(start, KEY_BLOCK), width:2 * width]
        pv = jnp.dot(p.astype(jnp.bfloat16), v, preferred_element_type=jnp.float32)
        acc_ref[lo:lo + count, :] = acc_ref[lo:lo + count, :] * rescale + pv
        top_ref[lo:lo + count, :] = new_top

    def fwd_both(block, carry):
        forward_block(0, rows, block)
        return carry

    def fwd_late(block, carry):
        forward_block(half, half, block)
        return carry

    lax.fori_loop(0, early_blocks, fwd_both, 0)
    lax.fori_loop(early_blocks, late_blocks, fwd_late, 0)

    attention = (acc_ref[...] / total_ref[...]).astype(jnp.bfloat16)
    out_ref[...] = attention
    lse_ref[...] = top_ref[...] + jnp.log(total_ref[...])
    dot_ref[...] = jnp.sum(
        g_ref[...].astype(jnp.float32) * attention.astype(jnp.float32), axis=1, keepdims=True
    )
    dqacc_ref[...] = jnp.zeros(dqacc_ref.shape, jnp.float32)
    dkv_ref[...] = jnp.zeros(dkv_ref.shape, jnp.float32)

    def backward_block(lo, count, block):
        start = pl.multiple_of(block * KEY_BLOCK, KEY_BLOCK)
        s, visible = scores_of(lo, count, start)
        probs = jnp.where(visible, jnp.exp(s - lse_ref[lo:lo + count, :]), 0.0)
        g = g_ref[lo:lo + count, :]
        k = kv_ref[pl.ds(start, KEY_BLOCK), 0:width]
        v = kv_ref[pl.ds(start, KEY_BLOCK), width:2 * width]
        grad_probs = lax.dot_general(g, v, (((1,), (1,)), ((), ())), preferred_element_type=jnp.float32)
        grad_scores = (probs * (grad_probs - dot_ref[lo:lo + count, :])).astype(jnp.bfloat16)
        dqacc_ref[lo:lo + count, :] += jnp.dot(grad_scores, k, preferred_element_type=jnp.float32)
        q = q_ref[lo:lo + count, :]
        dk = lax.dot_general(grad_scores, q, (((0,), (0,)), ((), ())), preferred_element_type=jnp.float32)
        dv = lax.dot_general(
            probs.astype(jnp.bfloat16), g, (((0,), (0,)), ((), ())), preferred_element_type=jnp.float32
        )
        dkv_ref[pl.ds(start, KEY_BLOCK), 0:width] += dk
        dkv_ref[pl.ds(start, KEY_BLOCK), width:2 * width] += dv

    def bwd_both(block, carry):
        backward_block(0, rows, block)
        return carry

    def bwd_late(block, carry):
        backward_block(half, half, block)
        return carry

    lax.fori_loop(0, early_blocks, bwd_both, 0)
    lax.fori_loop(early_blocks, late_blocks, bwd_late, 0)
    dq_ref[...] = (dqacc_ref[...] * scale).astype(jnp.bfloat16)


def local_attention(limits, q_rows, g_rows, kv_sorted, q_pos):
    rows, width = q_rows.shape
    keys = kv_sorted.shape[0]
    vmem = pltpu.VMEM
    flops = 2 * rows * keys * width * 7 // 2
    return pl.pallas_call(
        attention_kernel,
        out_shape=(
            jax.ShapeDtypeStruct((rows, width), jnp.bfloat16),
            jax.ShapeDtypeStruct((rows, width), jnp.bfloat16),
            jax.ShapeDtypeStruct((keys, 2 * width), jnp.float32),
        ),
        in_specs=[
            pl.BlockSpec(memory_space=pltpu.SMEM),
            pl.BlockSpec(memory_space=vmem),
            pl.BlockSpec(memory_space=vmem),
            pl.BlockSpec(memory_space=vmem),
            pl.BlockSpec(memory_space=vmem),
        ],
        out_specs=(
            pl.BlockSpec(memory_space=vmem),
            pl.BlockSpec(memory_space=vmem),
            pl.BlockSpec(memory_space=vmem),
        ),
        scratch_shapes=[
            pltpu.VMEM((rows, 1), jnp.float32),
            pltpu.VMEM((rows, 1), jnp.float32),
            pltpu.VMEM((rows, width), jnp.float32),
            pltpu.VMEM((rows, 1), jnp.float32),
            pltpu.VMEM((rows, 1), jnp.float32),
            pltpu.VMEM((rows, width), jnp.float32),
        ],
        cost_estimate=pl.CostEstimate(
            flops=flops, transcendentals=rows * keys, bytes_accessed=keys * width * 12
        ),
    )(limits, q_rows, g_rows, kv_sorted, q_pos)


def on_device(queries, keys, values, out_grad, order):
    row_count = queries.shape[0]
    width = HEAD_DIM
    score_scale = 1.0 / math.sqrt(width)
    cycle_size = lax.axis_size(CTX)
    span_count = 2 * cycle_size
    my_index = lax.axis_index(CTX)
    q_heads = queries.shape[1] // width

    outer = lax.axis_size("zh")
    inner = lax.axis_size("y")
    kv_local = jnp.concatenate([keys, values], axis=1)
    kv_all = lax.all_gather(lax.all_gather(kv_local, "zh", axis=0, tiled=True), "y", axis=0, tiled=True)
    kv_all = kv_all.reshape(inner, outer, 2 * SPAN, 2 * width).transpose(1, 0, 2, 3)
    inverse = jnp.zeros((span_count,), jnp.int32).at[order].set(jnp.arange(span_count, dtype=jnp.int32))
    kv_sorted = kv_all.reshape(span_count, SPAN, 2 * width)[inverse].reshape(span_count * SPAN, 2 * width)

    pair = lax.dynamic_slice_in_dim(order, 2 * my_index, 2)
    low_first = pair[0] < pair[1]
    my_low = jnp.minimum(pair[0], pair[1])
    early_keys = (my_low + 1) * SPAN
    late_keys = (span_count - my_low) * SPAN
    limits = jnp.stack(
        [(early_keys + KEY_BLOCK - 1) // KEY_BLOCK, (late_keys + KEY_BLOCK - 1) // KEY_BLOCK]
    ).astype(jnp.int32)

    def to_rows(array):
        blocks = array.reshape(2, SPAN, q_heads, width)
        blocks = jnp.where(low_first, blocks, blocks[::-1])
        return blocks.transpose(0, 2, 1, 3).reshape(2 * q_heads * SPAN, width)

    def from_rows(array):
        blocks = array.reshape(2, q_heads, SPAN, width).transpose(0, 2, 1, 3)
        blocks = jnp.where(low_first, blocks, blocks[::-1])
        return blocks.reshape(row_count, q_heads * width)

    offsets = jnp.arange(SPAN, dtype=jnp.int32)
    span_pos = jnp.stack([my_low, span_count - 1 - my_low])[:, None] * SPAN + offsets[None, :]
    q_pos = jnp.broadcast_to(span_pos[:, None, :], (2, q_heads, SPAN)).reshape(-1, 1)

    attention_rows, dq_rows, dkv_sorted = local_attention(
        limits, to_rows(queries), to_rows(out_grad), kv_sorted, q_pos
    )
    dkv_all = dkv_sorted.reshape(span_count, SPAN, 2 * width)[order].reshape(outer, inner, 2 * SPAN, 2 * width)
    row_parts = lax.all_to_all(dkv_all.astype(jnp.bfloat16), "y", 1, 1, tiled=False)
    row_sums = jnp.sum(row_parts.astype(jnp.float32), axis=1)
    dkv_parts = lax.all_to_all(row_sums.astype(jnp.bfloat16), "zh", 0, 0, tiled=False)
    dkv_mine = jnp.sum(dkv_parts.astype(jnp.float32), axis=0)
    grad_keys = (score_scale * dkv_mine[:, :width]).astype(jnp.bfloat16)
    grad_values = dkv_mine[:, width:].astype(jnp.bfloat16)
    return (from_rows(attention_rows), from_rows(dq_rows), grad_keys, grad_values)


def solution(mesh):
    ctx_size = mesh.shape["ctx"]
    outer = 4 if ctx_size % 4 == 0 else 1
    split = Mesh(
        mesh.devices.reshape(outer, ctx_size // outer, mesh.shape["head"]), ("zh", "y", "head")
    )
    rows = P(CTX, "head")
    return jax.shard_map(
        on_device,
        mesh=split,
        in_specs=(rows, rows, rows, rows, P()),
        out_specs=(rows, rows, rows, rows),
        check_vma=False,
    )
```

```python
import math

import jax
import jax.numpy as jnp
from jax import lax
from jax.experimental import pallas as pl
from jax.experimental.pallas import tpu as pltpu
from jax.sharding import Mesh
from jax.sharding import PartitionSpec as P

HEADS = 32
KV_HEADS = 8
HEAD_DIM = 128
SPAN = 80
KEY_BLOCK = 5120

NEG = -1e30
CTX = ("zh", "y")


def attention_kernel(
    limits_ref, q_ref, g_ref, kv_ref, qpos_ref,
    out_ref, dq_ref, dkv_ref,
    top_ref, total_ref, acc_ref, lse_ref, dot_ref, dqacc_ref,
):
    rows = q_ref.shape[0]
    half = rows // 2
    width = HEAD_DIM
    scale = 1.0 / math.sqrt(width)
    early_blocks = limits_ref[0]
    late_blocks = limits_ref[1]

    top_ref[...] = jnp.full(top_ref.shape, NEG, jnp.float32)
    total_ref[...] = jnp.zeros(total_ref.shape, jnp.float32)
    acc_ref[...] = jnp.zeros(acc_ref.shape, jnp.float32)

    def scores_of(lo, count, start):
        q = q_ref[lo:lo + count, :]
        k = kv_ref[pl.ds(start, KEY_BLOCK), 0:width]
        s = lax.dot_general(q, k, (((1,), (1,)), ((), ())), preferred_element_type=jnp.float32) * scale
        kpos = start + lax.broadcasted_iota(jnp.int32, (1, KEY_BLOCK), 1)
        visible = kpos <= qpos_ref[lo:lo + count, :]
        return s, visible

    def forward_block(lo, count, block):
        start = pl.multiple_of(block * KEY_BLOCK, KEY_BLOCK)
        s, visible = scores_of(lo, count, start)
        s = jnp.where(visible, s, NEG)
        old_top = top_ref[lo:lo + count, :]
        new_top = jnp.maximum(old_top, jnp.max(s, axis=1, keepdims=True))
        p = jnp.where(visible, jnp.exp(s - new_top), 0.0)
        rescale = jnp.exp(old_top - new_top)
        total_ref[lo:lo + count, :] = total_ref[lo:lo + count, :] * rescale + jnp.sum(p, axis=1, keepdims=True)
        v = kv_ref[pl.ds(start, KEY_BLOCK), width:2 * width]
        pv = jnp.dot(p.astype(jnp.bfloat16), v, preferred_element_type=jnp.float32)
        acc_ref[lo:lo + count, :] = acc_ref[lo:lo + count, :] * rescale + pv
        top_ref[lo:lo + count, :] = new_top

    def fwd_both(block, carry):
        forward_block(0, rows, block)
        return carry

    def fwd_late(block, carry):
        forward_block(half, half, block)
        return carry

    lax.fori_loop(0, early_blocks, fwd_both, 0)
    lax.fori_loop(early_blocks, late_blocks, fwd_late, 0)

    attention = (acc_ref[...] / total_ref[...]).astype(jnp.bfloat16)
    out_ref[...] = attention
    lse_ref[...] = top_ref[...] + jnp.log(total_ref[...])
    dot_ref[...] = jnp.sum(
        g_ref[...].astype(jnp.float32) * attention.astype(jnp.float32), axis=1, keepdims=True
    )
    dqacc_ref[...] = jnp.zeros(dqacc_ref.shape, jnp.float32)
    dkv_ref[...] = jnp.zeros(dkv_ref.shape, jnp.float32)

    def backward_block(lo, count, block):
        start = pl.multiple_of(block * KEY_BLOCK, KEY_BLOCK)
        s, visible = scores_of(lo, count, start)
        probs = jnp.where(visible, jnp.exp(s - lse_ref[lo:lo + count, :]), 0.0)
        g = g_ref[lo:lo + count, :]
        k = kv_ref[pl.ds(start, KEY_BLOCK), 0:width]
        v = kv_ref[pl.ds(start, KEY_BLOCK), width:2 * width]
        grad_probs = lax.dot_general(g, v, (((1,), (1,)), ((), ())), preferred_element_type=jnp.float32)
        grad_scores = (probs * (grad_probs - dot_ref[lo:lo + count, :])).astype(jnp.bfloat16)
        dqacc_ref[lo:lo + count, :] += jnp.dot(grad_scores, k, preferred_element_type=jnp.float32)
        q = q_ref[lo:lo + count, :]
        dk = lax.dot_general(grad_scores, q, (((0,), (0,)), ((), ())), preferred_element_type=jnp.float32)
        dv = lax.dot_general(
            probs.astype(jnp.bfloat16), g, (((0,), (0,)), ((), ())), preferred_element_type=jnp.float32
        )
        dkv_ref[pl.ds(start, KEY_BLOCK), 0:width] += dk
        dkv_ref[pl.ds(start, KEY_BLOCK), width:2 * width] += dv

    def bwd_both(block, carry):
        backward_block(0, rows, block)
        return carry

    def bwd_late(block, carry):
        backward_block(half, half, block)
        return carry

    lax.fori_loop(0, early_blocks, bwd_both, 0)
    lax.fori_loop(early_blocks, late_blocks, bwd_late, 0)
    dq_ref[...] = (dqacc_ref[...] * scale).astype(jnp.bfloat16)


def local_attention(limits, q_rows, g_rows, kv_sorted, q_pos):
    rows, width = q_rows.shape
    keys = kv_sorted.shape[0]
    vmem = pltpu.VMEM
    flops = 2 * rows * keys * width * 7 // 2
    return pl.pallas_call(
        attention_kernel,
        out_shape=(
            jax.ShapeDtypeStruct((rows, width), jnp.bfloat16),
            jax.ShapeDtypeStruct((rows, width), jnp.bfloat16),
            jax.ShapeDtypeStruct((keys, 2 * width), jnp.float32),
        ),
        in_specs=[
            pl.BlockSpec(memory_space=pltpu.SMEM),
            pl.BlockSpec(memory_space=vmem),
            pl.BlockSpec(memory_space=vmem),
            pl.BlockSpec(memory_space=vmem),
            pl.BlockSpec(memory_space=vmem),
        ],
        out_specs=(
            pl.BlockSpec(memory_space=vmem),
            pl.BlockSpec(memory_space=vmem),
            pl.BlockSpec(memory_space=vmem),
        ),
        scratch_shapes=[
            pltpu.VMEM((rows, 1), jnp.float32),
            pltpu.VMEM((rows, 1), jnp.float32),
            pltpu.VMEM((rows, width), jnp.float32),
            pltpu.VMEM((rows, 1), jnp.float32),
            pltpu.VMEM((rows, 1), jnp.float32),
            pltpu.VMEM((rows, width), jnp.float32),
        ],
        cost_estimate=pl.CostEstimate(
            flops=flops, transcendentals=rows * keys, bytes_accessed=keys * width * 12
        ),
    )(limits, q_rows, g_rows, kv_sorted, q_pos)


def on_device(queries, keys, values, out_grad, order):
    row_count = queries.shape[0]
    width = HEAD_DIM
    score_scale = 1.0 / math.sqrt(width)
    cycle_size = lax.axis_size(CTX)
    span_count = 2 * cycle_size
    my_index = lax.axis_index(CTX)
    q_heads = queries.shape[1] // width

    outer = lax.axis_size("zh")
    inner = lax.axis_size("y")
    kv_local = jnp.concatenate([keys, values], axis=1)
    kv_all = lax.all_gather(lax.all_gather(kv_local, "zh", axis=0, tiled=True), "y", axis=0, tiled=True)
    kv_all = kv_all.reshape(inner, outer, 2 * SPAN, 2 * width).transpose(1, 0, 2, 3)
    inverse = jnp.zeros((span_count,), jnp.int32).at[order].set(jnp.arange(span_count, dtype=jnp.int32))
    kv_sorted = kv_all.reshape(span_count, SPAN, 2 * width)[inverse].reshape(span_count * SPAN, 2 * width)

    pair = lax.dynamic_slice_in_dim(order, 2 * my_index, 2)
    low_first = pair[0] < pair[1]
    my_low = jnp.minimum(pair[0], pair[1])
    early_keys = (my_low + 1) * SPAN
    late_keys = (span_count - my_low) * SPAN
    limits = jnp.stack(
        [(early_keys + KEY_BLOCK - 1) // KEY_BLOCK, (late_keys + KEY_BLOCK - 1) // KEY_BLOCK]
    ).astype(jnp.int32)

    def to_rows(array):
        blocks = array.reshape(2, SPAN, q_heads, width)
        blocks = jnp.where(low_first, blocks, blocks[::-1])
        return blocks.transpose(0, 2, 1, 3).reshape(2 * q_heads * SPAN, width)

    def from_rows(array):
        blocks = array.reshape(2, q_heads, SPAN, width).transpose(0, 2, 1, 3)
        blocks = jnp.where(low_first, blocks, blocks[::-1])
        return blocks.reshape(row_count, q_heads * width)

    offsets = jnp.arange(SPAN, dtype=jnp.int32)
    span_pos = jnp.stack([my_low, span_count - 1 - my_low])[:, None] * SPAN + offsets[None, :]
    q_pos = jnp.broadcast_to(span_pos[:, None, :], (2, q_heads, SPAN)).reshape(-1, 1)

    attention_rows, dq_rows, dkv_sorted = local_attention(
        limits, to_rows(queries), to_rows(out_grad), kv_sorted, q_pos
    )
    dkv_all = dkv_sorted.reshape(span_count, SPAN, 2 * width)[order].reshape(outer, inner, 2 * SPAN, 2 * width)
    row_parts = lax.all_to_all(dkv_all.astype(jnp.bfloat16), "y", 1, 1, tiled=False)
    row_sums = jnp.sum(row_parts.astype(jnp.float32), axis=1)
    dkv_parts = lax.all_to_all(row_sums.astype(jnp.bfloat16), "zh", 0, 0, tiled=False)
    dkv_mine = jnp.sum(dkv_parts.astype(jnp.float32), axis=0)
    grad_keys = (score_scale * dkv_mine[:, :width]).astype(jnp.bfloat16)
    grad_values = dkv_mine[:, width:].astype(jnp.bfloat16)
    return (from_rows(attention_rows), from_rows(dq_rows), grad_keys, grad_values)


def solution(mesh):
    ctx_size = mesh.shape["ctx"]
    outer = 4 if ctx_size % 4 == 0 else 1
    split = Mesh(
        mesh.devices.reshape(outer, ctx_size // outer, mesh.shape["head"]), ("zh", "y", "head")
    )
    rows = P(CTX, "head")
    return jax.shard_map(
        on_device,
        mesh=split,
        in_specs=(rows, rows, rows, rows, P()),
        out_specs=(rows, rows, rows, rows),
        check_vma=False,
    )
```

```python
import math

import jax
import jax.numpy as jnp
from jax import lax
from jax.experimental import pallas as pl
from jax.experimental.pallas import tpu as pltpu
from jax.sharding import Mesh
from jax.sharding import PartitionSpec as P

HEADS = 32
KV_HEADS = 8
HEAD_DIM = 128
SPAN = 80
KEY_BLOCK = 1024

NEG = -1e30
CTX = ("zh", "y")


def attention_kernel(
    limits_ref, q_ref, g_ref, kv_ref, qpos_ref,
    out_ref, dq_ref, dkv_ref,
    top_ref, total_ref, acc_ref, lse_ref, dot_ref, dqacc_ref,
):
    rows = q_ref.shape[0]
    half = rows // 2
    width = HEAD_DIM
    scale = 1.0 / math.sqrt(width)
    early_blocks = limits_ref[0]
    late_blocks = limits_ref[1]
    early_first = limits_ref[2]
    late_first = limits_ref[3]

    top_ref[...] = jnp.full(top_ref.shape, NEG, jnp.float32)
    total_ref[...] = jnp.zeros(total_ref.shape, jnp.float32)
    acc_ref[...] = jnp.zeros(acc_ref.shape, jnp.float32)

    def scores_of(lo, count, start, masked):
        q = q_ref[lo:lo + count, :]
        k = kv_ref[pl.ds(start, KEY_BLOCK), 0:width]
        s = lax.dot_general(q, k, (((1,), (1,)), ((), ())), preferred_element_type=jnp.float32) * scale
        if masked:
            kpos = start + lax.broadcasted_iota(jnp.int32, (1, KEY_BLOCK), 1)
            s = jnp.where(kpos <= qpos_ref[lo:lo + count, :], s, NEG)
        return s

    def forward_masked(lo, count, start, masked):
        s = scores_of(lo, count, start, masked)
        old_top = top_ref[lo:lo + count, :]
        new_top = jnp.maximum(old_top, jnp.max(s, axis=1, keepdims=True))
        p = jnp.exp(s - new_top)
        rescale = jnp.exp(old_top - new_top)
        total_ref[lo:lo + count, :] = total_ref[lo:lo + count, :] * rescale + jnp.sum(p, axis=1, keepdims=True)
        v = kv_ref[pl.ds(start, KEY_BLOCK), width:2 * width]
        pv = jnp.dot(p.astype(jnp.bfloat16), v, preferred_element_type=jnp.float32)
        acc_ref[lo:lo + count, :] = acc_ref[lo:lo + count, :] * rescale + pv
        top_ref[lo:lo + count, :] = new_top

    def split_by_mask(body, lo, count, block, first_row):
        start = pl.multiple_of(block * KEY_BLOCK, KEY_BLOCK)
        needs_mask = start + KEY_BLOCK - 1 > first_row

        @pl.when(needs_mask)
        def _():
            body(lo, count, start, True)

        @pl.when(jnp.logical_not(needs_mask))
        def _():
            body(lo, count, start, False)

    def forward_block(lo, count, block, first_row):
        split_by_mask(forward_masked, lo, count, block, first_row)

    def fwd_both(block, carry):
        forward_block(0, rows, block, early_first)
        return carry

    def fwd_late(block, carry):
        forward_block(half, half, block, late_first)
        return carry

    lax.fori_loop(0, early_blocks, fwd_both, 0)
    lax.fori_loop(early_blocks, late_blocks, fwd_late, 0)

    attention = (acc_ref[...] / total_ref[...]).astype(jnp.bfloat16)
    out_ref[...] = attention
    lse_ref[...] = top_ref[...] + jnp.log(total_ref[...])
    dot_ref[...] = jnp.sum(
        g_ref[...].astype(jnp.float32) * attention.astype(jnp.float32), axis=1, keepdims=True
    )
    dqacc_ref[...] = jnp.zeros(dqacc_ref.shape, jnp.float32)
    dkv_ref[...] = jnp.zeros(dkv_ref.shape, jnp.float32)

    def backward_masked(lo, count, start, masked):
        s = scores_of(lo, count, start, masked)
        probs = jnp.exp(s - lse_ref[lo:lo + count, :])
        g = g_ref[lo:lo + count, :]
        k = kv_ref[pl.ds(start, KEY_BLOCK), 0:width]
        v = kv_ref[pl.ds(start, KEY_BLOCK), width:2 * width]
        grad_probs = lax.dot_general(g, v, (((1,), (1,)), ((), ())), preferred_element_type=jnp.float32)
        grad_scores = (probs * (grad_probs - dot_ref[lo:lo + count, :])).astype(jnp.bfloat16)
        dqacc_ref[lo:lo + count, :] += jnp.dot(grad_scores, k, preferred_element_type=jnp.float32)
        q = q_ref[lo:lo + count, :]
        dk = lax.dot_general(grad_scores, q, (((0,), (0,)), ((), ())), preferred_element_type=jnp.float32)
        dv = lax.dot_general(
            probs.astype(jnp.bfloat16), g, (((0,), (0,)), ((), ())), preferred_element_type=jnp.float32
        )
        dkv_ref[pl.ds(start, KEY_BLOCK), 0:width] += dk
        dkv_ref[pl.ds(start, KEY_BLOCK), width:2 * width] += dv

    def bwd_both(block, carry):
        split_by_mask(backward_masked, 0, rows, block, early_first)
        return carry

    def bwd_late(block, carry):
        split_by_mask(backward_masked, half, half, block, late_first)
        return carry

    lax.fori_loop(0, early_blocks, bwd_both, 0)
    lax.fori_loop(early_blocks, late_blocks, bwd_late, 0)
    dq_ref[...] = (dqacc_ref[...] * scale).astype(jnp.bfloat16)


def local_attention(limits, q_rows, g_rows, kv_sorted, q_pos):
    rows, width = q_rows.shape
    keys = kv_sorted.shape[0]
    vmem = pltpu.VMEM
    flops = 2 * rows * keys * width * 7 // 2
    return pl.pallas_call(
        attention_kernel,
        out_shape=(
            jax.ShapeDtypeStruct((rows, width), jnp.bfloat16),
            jax.ShapeDtypeStruct((rows, width), jnp.bfloat16),
            jax.ShapeDtypeStruct((keys, 2 * width), jnp.float32),
        ),
        in_specs=[
            pl.BlockSpec(memory_space=pltpu.SMEM),
            pl.BlockSpec(memory_space=vmem),
            pl.BlockSpec(memory_space=vmem),
            pl.BlockSpec(memory_space=vmem),
            pl.BlockSpec(memory_space=vmem),
        ],
        out_specs=(
            pl.BlockSpec(memory_space=vmem),
            pl.BlockSpec(memory_space=vmem),
            pl.BlockSpec(memory_space=vmem),
        ),
        scratch_shapes=[
            pltpu.VMEM((rows, 1), jnp.float32),
            pltpu.VMEM((rows, 1), jnp.float32),
            pltpu.VMEM((rows, width), jnp.float32),
            pltpu.VMEM((rows, 1), jnp.float32),
            pltpu.VMEM((rows, 1), jnp.float32),
            pltpu.VMEM((rows, width), jnp.float32),
        ],
        cost_estimate=pl.CostEstimate(
            flops=flops, transcendentals=rows * keys, bytes_accessed=keys * width * 12
        ),
    )(limits, q_rows, g_rows, kv_sorted, q_pos)


def on_device(queries, keys, values, out_grad, order):
    row_count = queries.shape[0]
    width = HEAD_DIM
    score_scale = 1.0 / math.sqrt(width)
    cycle_size = lax.axis_size(CTX)
    span_count = 2 * cycle_size
    my_index = lax.axis_index(CTX)
    q_heads = queries.shape[1] // width

    outer = lax.axis_size("zh")
    inner = lax.axis_size("y")
    kv_local = jnp.concatenate([keys, values], axis=1)
    kv_all = lax.all_gather(lax.all_gather(kv_local, "zh", axis=0, tiled=True), "y", axis=0, tiled=True)
    inverse = jnp.zeros((span_count,), jnp.int32).at[order].set(jnp.arange(span_count, dtype=jnp.int32))
    holder = inverse // 2
    gathered_at = 2 * ((holder % inner) * outer + holder // inner) + inverse % 2
    kv_sorted = kv_all.reshape(span_count, SPAN, 2 * width)[gathered_at].reshape(span_count * SPAN, 2 * width)

    pair = lax.dynamic_slice_in_dim(order, 2 * my_index, 2)
    low_first = pair[0] < pair[1]
    my_low = jnp.minimum(pair[0], pair[1])
    early_keys = (my_low + 1) * SPAN
    late_keys = (span_count - my_low) * SPAN
    limits = jnp.stack(
        [
            (early_keys + KEY_BLOCK - 1) // KEY_BLOCK,
            (late_keys + KEY_BLOCK - 1) // KEY_BLOCK,
            my_low * SPAN,
            (span_count - 1 - my_low) * SPAN,
        ]
    ).astype(jnp.int32)

    def to_rows(array):
        blocks = array.reshape(2, SPAN, q_heads, width)
        blocks = jnp.where(low_first, blocks, blocks[::-1])
        return blocks.transpose(0, 2, 1, 3).reshape(2 * q_heads * SPAN, width)

    def from_rows(array):
        blocks = array.reshape(2, q_heads, SPAN, width).transpose(0, 2, 1, 3)
        blocks = jnp.where(low_first, blocks, blocks[::-1])
        return blocks.reshape(row_count, q_heads * width)

    offsets = jnp.arange(SPAN, dtype=jnp.int32)
    span_pos = jnp.stack([my_low, span_count - 1 - my_low])[:, None] * SPAN + offsets[None, :]
    q_pos = jnp.broadcast_to(span_pos[:, None, :], (2, q_heads, SPAN)).reshape(-1, 1)

    attention_rows, dq_rows, dkv_sorted = local_attention(
        limits, to_rows(queries), to_rows(out_grad), kv_sorted, q_pos
    )
    dkv_all = dkv_sorted.reshape(span_count, SPAN, 2 * width)[order].reshape(outer, inner, 2 * SPAN, 2 * width)
    row_parts = lax.all_to_all(dkv_all.astype(jnp.bfloat16), "y", 1, 1, tiled=False)
    row_sums = jnp.sum(row_parts.astype(jnp.float32), axis=1)
    dkv_parts = lax.all_to_all(row_sums.astype(jnp.bfloat16), "zh", 0, 0, tiled=False)
    dkv_mine = jnp.sum(dkv_parts.astype(jnp.float32), axis=0)
    grad_keys = (score_scale * dkv_mine[:, :width]).astype(jnp.bfloat16)
    grad_values = dkv_mine[:, width:].astype(jnp.bfloat16)
    return (from_rows(attention_rows), from_rows(dq_rows), grad_keys, grad_values)


def solution(mesh):
    ctx_size = mesh.shape["ctx"]
    outer = 4 if ctx_size % 4 == 0 else 1
    split = Mesh(
        mesh.devices.reshape(outer, ctx_size // outer, mesh.shape["head"]), ("zh", "y", "head")
    )
    rows = P(CTX, "head")
    return jax.shard_map(
        on_device,
        mesh=split,
        in_specs=(rows, rows, rows, rows, P()),
        out_specs=(rows, rows, rows, rows),
        check_vma=False,
    )
```

```python
import math

import jax
import jax.numpy as jnp
from jax import lax
from jax.experimental import pallas as pl
from jax.experimental.pallas import tpu as pltpu
from jax.sharding import Mesh
from jax.sharding import PartitionSpec as P

HEADS = 32
KV_HEADS = 8
HEAD_DIM = 128
SPAN = 80
KEY_BLOCK = 1024

NEG = -1e30
CTX = ("zh", "y")


def attention_kernel(
    limits_ref, q_ref, g_ref, kv_ref, qpos_ref,
    out_ref, dq_ref, dkv_ref,
    top_ref, total_ref, acc_ref, lse_ref, dot_ref, dqacc_ref,
):
    rows = q_ref.shape[0]
    half = rows // 2
    width = HEAD_DIM
    scale = 1.0 / math.sqrt(width)
    early_blocks = limits_ref[0]
    late_blocks = limits_ref[1]
    early_first = limits_ref[2]
    late_first = limits_ref[3]

    top_ref[...] = jnp.full(top_ref.shape, NEG, jnp.float32)
    total_ref[...] = jnp.zeros(total_ref.shape, jnp.float32)
    acc_ref[...] = jnp.zeros(acc_ref.shape, jnp.float32)

    def scores_of(lo, count, start, masked):
        q = q_ref[lo:lo + count, :]
        k = kv_ref[pl.ds(start, KEY_BLOCK), 0:width]
        s = lax.dot_general(q, k, (((1,), (1,)), ((), ())), preferred_element_type=jnp.float32) * scale
        if masked:
            kpos = start + lax.broadcasted_iota(jnp.int32, (1, KEY_BLOCK), 1)
            s = jnp.where(kpos <= qpos_ref[lo:lo + count, :], s, NEG)
        return s

    def forward_masked(lo, count, start, masked):
        s = scores_of(lo, count, start, masked)
        old_top = top_ref[lo:lo + count, :]
        new_top = jnp.maximum(old_top, jnp.max(s, axis=1, keepdims=True))
        p = jnp.exp(s - new_top)
        rescale = jnp.exp(old_top - new_top)
        total_ref[lo:lo + count, :] = total_ref[lo:lo + count, :] * rescale + jnp.sum(p, axis=1, keepdims=True)
        v = kv_ref[pl.ds(start, KEY_BLOCK), width:2 * width]
        pv = jnp.dot(p.astype(jnp.bfloat16), v, preferred_element_type=jnp.float32)
        acc_ref[lo:lo + count, :] = acc_ref[lo:lo + count, :] * rescale + pv
        top_ref[lo:lo + count, :] = new_top

    def split_by_mask(body, lo, count, block, first_row):
        start = pl.multiple_of(block * KEY_BLOCK, KEY_BLOCK)
        needs_mask = start + KEY_BLOCK - 1 > first_row

        @pl.when(needs_mask)
        def _():
            body(lo, count, start, True)

        @pl.when(jnp.logical_not(needs_mask))
        def _():
            body(lo, count, start, False)

    def forward_block(lo, count, block, first_row):
        split_by_mask(forward_masked, lo, count, block, first_row)

    def fwd_both(block, carry):
        forward_block(0, rows, block, early_first)
        return carry

    def fwd_late(block, carry):
        forward_block(half, half, block, late_first)
        return carry

    lax.fori_loop(0, early_blocks, fwd_both, 0)
    lax.fori_loop(early_blocks, late_blocks, fwd_late, 0)

    attention = (acc_ref[...] / total_ref[...]).astype(jnp.bfloat16)
    out_ref[...] = attention
    lse_ref[...] = top_ref[...] + jnp.log(total_ref[...])
    dot_ref[...] = jnp.sum(
        g_ref[...].astype(jnp.float32) * attention.astype(jnp.float32), axis=1, keepdims=True
    )
    dqacc_ref[...] = jnp.zeros(dqacc_ref.shape, jnp.float32)
    dkv_ref[...] = jnp.zeros(dkv_ref.shape, jnp.float32)

    def backward_masked(lo, count, start, masked):
        s = scores_of(lo, count, start, masked)
        probs = jnp.exp(s - lse_ref[lo:lo + count, :])
        g = g_ref[lo:lo + count, :]
        k = kv_ref[pl.ds(start, KEY_BLOCK), 0:width]
        v = kv_ref[pl.ds(start, KEY_BLOCK), width:2 * width]
        grad_probs = lax.dot_general(g, v, (((1,), (1,)), ((), ())), preferred_element_type=jnp.float32)
        grad_scores = (probs * (grad_probs - dot_ref[lo:lo + count, :])).astype(jnp.bfloat16)
        dqacc_ref[lo:lo + count, :] += jnp.dot(grad_scores, k, preferred_element_type=jnp.float32)
        q = q_ref[lo:lo + count, :]
        dk = lax.dot_general(grad_scores, q, (((0,), (0,)), ((), ())), preferred_element_type=jnp.float32)
        dv = lax.dot_general(
            probs.astype(jnp.bfloat16), g, (((0,), (0,)), ((), ())), preferred_element_type=jnp.float32
        )
        dkv_ref[pl.ds(start, KEY_BLOCK), 0:width] += dk
        dkv_ref[pl.ds(start, KEY_BLOCK), width:2 * width] += dv

    def bwd_both(block, carry):
        split_by_mask(backward_masked, 0, rows, block, early_first)
        return carry

    def bwd_late(block, carry):
        split_by_mask(backward_masked, half, half, block, late_first)
        return carry

    lax.fori_loop(0, early_blocks, bwd_both, 0)
    lax.fori_loop(early_blocks, late_blocks, bwd_late, 0)
    dq_ref[...] = (dqacc_ref[...] * scale).astype(jnp.bfloat16)


def shifted(array, axis, by):
    length = lax.axis_size(axis)
    return lax.ppermute(array, axis, [(i, (i + by) % length) for i in range(length)])


def local_attention(limits, q_rows, g_rows, kv_sorted, q_pos):
    rows, width = q_rows.shape
    keys = kv_sorted.shape[0]
    vmem = pltpu.VMEM
    flops = 2 * rows * keys * width * 7 // 2
    return pl.pallas_call(
        attention_kernel,
        out_shape=(
            jax.ShapeDtypeStruct((rows, width), jnp.bfloat16),
            jax.ShapeDtypeStruct((rows, width), jnp.bfloat16),
            jax.ShapeDtypeStruct((keys, 2 * width), jnp.float32),
        ),
        in_specs=[
            pl.BlockSpec(memory_space=pltpu.SMEM),
            pl.BlockSpec(memory_space=vmem),
            pl.BlockSpec(memory_space=vmem),
            pl.BlockSpec(memory_space=vmem),
            pl.BlockSpec(memory_space=vmem),
        ],
        out_specs=(
            pl.BlockSpec(memory_space=vmem),
            pl.BlockSpec(memory_space=vmem),
            pl.BlockSpec(memory_space=vmem),
        ),
        scratch_shapes=[
            pltpu.VMEM((rows, 1), jnp.float32),
            pltpu.VMEM((rows, 1), jnp.float32),
            pltpu.VMEM((rows, width), jnp.float32),
            pltpu.VMEM((rows, 1), jnp.float32),
            pltpu.VMEM((rows, 1), jnp.float32),
            pltpu.VMEM((rows, width), jnp.float32),
        ],
        cost_estimate=pl.CostEstimate(
            flops=flops, transcendentals=rows * keys, bytes_accessed=keys * width * 12
        ),
    )(limits, q_rows, g_rows, kv_sorted, q_pos)


def on_device(queries, keys, values, out_grad, order):
    row_count = queries.shape[0]
    width = HEAD_DIM
    score_scale = 1.0 / math.sqrt(width)
    cycle_size = lax.axis_size(CTX)
    span_count = 2 * cycle_size
    my_index = lax.axis_index(CTX)
    q_heads = queries.shape[1] // width

    outer = lax.axis_size("zh")
    inner = lax.axis_size("y")
    kv_local = jnp.concatenate([keys, values], axis=1)
    column = lax.all_gather(kv_local, "zh", axis=0, tiled=True)
    rightward = [column]
    leftward = [column]
    for _ in range(inner // 2):
        rightward.append(shifted(rightward[-1], "y", 1))
    for _ in range((inner - 1) // 2):
        leftward.append(shifted(leftward[-1], "y", -1))
    by_distance = leftward + rightward[1:][::-1]
    kv_all = jnp.concatenate(by_distance, axis=0)
    my_y = lax.axis_index("y")
    inverse = jnp.zeros((span_count,), jnp.int32).at[order].set(jnp.arange(span_count, dtype=jnp.int32))
    holder = inverse // 2
    distance = (holder % inner - my_y + inner) % inner
    gathered_at = 2 * (distance * outer + holder // inner) + inverse % 2
    kv_sorted = kv_all.reshape(span_count, SPAN, 2 * width)[gathered_at].reshape(span_count * SPAN, 2 * width)

    pair = lax.dynamic_slice_in_dim(order, 2 * my_index, 2)
    low_first = pair[0] < pair[1]
    my_low = jnp.minimum(pair[0], pair[1])
    early_keys = (my_low + 1) * SPAN
    late_keys = (span_count - my_low) * SPAN
    limits = jnp.stack(
        [
            (early_keys + KEY_BLOCK - 1) // KEY_BLOCK,
            (late_keys + KEY_BLOCK - 1) // KEY_BLOCK,
            my_low * SPAN,
            (span_count - 1 - my_low) * SPAN,
        ]
    ).astype(jnp.int32)

    def to_rows(array):
        blocks = array.reshape(2, SPAN, q_heads, width)
        blocks = jnp.where(low_first, blocks, blocks[::-1])
        return blocks.transpose(0, 2, 1, 3).reshape(2 * q_heads * SPAN, width)

    def from_rows(array):
        blocks = array.reshape(2, q_heads, SPAN, width).transpose(0, 2, 1, 3)
        blocks = jnp.where(low_first, blocks, blocks[::-1])
        return blocks.reshape(row_count, q_heads * width)

    offsets = jnp.arange(SPAN, dtype=jnp.int32)
    span_pos = jnp.stack([my_low, span_count - 1 - my_low])[:, None] * SPAN + offsets[None, :]
    q_pos = jnp.broadcast_to(span_pos[:, None, :], (2, q_heads, SPAN)).reshape(-1, 1)

    attention_rows, dq_rows, dkv_sorted = local_attention(
        limits, to_rows(queries), to_rows(out_grad), kv_sorted, q_pos
    )
    dkv_all = dkv_sorted.reshape(span_count, SPAN, 2 * width)[order].reshape(outer, inner, 2 * SPAN, 2 * width)
    row_parts = lax.all_to_all(dkv_all.astype(jnp.bfloat16), "y", 1, 1, tiled=False)
    row_sums = jnp.sum(row_parts.astype(jnp.float32), axis=1)
    dkv_parts = lax.all_to_all(row_sums.astype(jnp.bfloat16), "zh", 0, 0, tiled=False)
    dkv_mine = jnp.sum(dkv_parts.astype(jnp.float32), axis=0)
    grad_keys = (score_scale * dkv_mine[:, :width]).astype(jnp.bfloat16)
    grad_values = dkv_mine[:, width:].astype(jnp.bfloat16)
    return (from_rows(attention_rows), from_rows(dq_rows), grad_keys, grad_values)


def solution(mesh):
    ctx_size = mesh.shape["ctx"]
    outer = 4 if ctx_size % 4 == 0 else 1
    split = Mesh(
        mesh.devices.reshape(outer, ctx_size // outer, mesh.shape["head"]), ("zh", "y", "head")
    )
    rows = P(CTX, "head")
    return jax.shard_map(
        on_device,
        mesh=split,
        in_specs=(rows, rows, rows, rows, P()),
        out_specs=(rows, rows, rows, rows),
        check_vma=False,
    )
```

```python
import math

import jax
import jax.numpy as jnp
from jax import lax
from jax.experimental import pallas as pl
from jax.experimental.pallas import tpu as pltpu
from jax.sharding import Mesh
from jax.sharding import PartitionSpec as P

HEADS = 32
KV_HEADS = 8
HEAD_DIM = 128
SPAN = 80
KEY_BLOCK = 1024

NEG = -1e30
CTX = ("zh", "y")


def attention_kernel(
    limits_ref, q_ref, g_ref, kv_ref, qpos_ref,
    out_ref, dq_ref, dkv_ref,
    top_ref, total_ref, acc_ref, lse_ref, dot_ref, dqacc_ref,
):
    rows = q_ref.shape[0]
    half = rows // 2
    width = HEAD_DIM
    scale = 1.0 / math.sqrt(width)
    early_blocks = limits_ref[0]
    late_blocks = limits_ref[1]
    early_first = limits_ref[2]
    late_first = limits_ref[3]

    top_ref[...] = jnp.full(top_ref.shape, NEG, jnp.float32)
    total_ref[...] = jnp.zeros(total_ref.shape, jnp.float32)
    acc_ref[...] = jnp.zeros(acc_ref.shape, jnp.float32)

    def scores_of(lo, count, start, masked):
        q = q_ref[lo:lo + count, :]
        k = kv_ref[pl.ds(start, KEY_BLOCK), 0:width]
        s = lax.dot_general(q, k, (((1,), (1,)), ((), ())), preferred_element_type=jnp.float32) * scale
        if masked:
            kpos = start + lax.broadcasted_iota(jnp.int32, (1, KEY_BLOCK), 1)
            s = jnp.where(kpos <= qpos_ref[lo:lo + count, :], s, NEG)
        return s

    def forward_masked(lo, count, start, masked):
        s = scores_of(lo, count, start, masked)
        old_top = top_ref[lo:lo + count, :]
        new_top = jnp.maximum(old_top, jnp.max(s, axis=1, keepdims=True))
        p = jnp.exp(s - new_top)
        rescale = jnp.exp(old_top - new_top)
        total_ref[lo:lo + count, :] = total_ref[lo:lo + count, :] * rescale + jnp.sum(p, axis=1, keepdims=True)
        v = kv_ref[pl.ds(start, KEY_BLOCK), width:2 * width]
        pv = jnp.dot(p.astype(jnp.bfloat16), v, preferred_element_type=jnp.float32)
        acc_ref[lo:lo + count, :] = acc_ref[lo:lo + count, :] * rescale + pv
        top_ref[lo:lo + count, :] = new_top

    def split_by_mask(body, lo, count, block, first_row):
        start = pl.multiple_of(block * KEY_BLOCK, KEY_BLOCK)
        needs_mask = start + KEY_BLOCK - 1 > first_row

        @pl.when(needs_mask)
        def _():
            body(lo, count, start, True)

        @pl.when(jnp.logical_not(needs_mask))
        def _():
            body(lo, count, start, False)

    def forward_block(lo, count, block, first_row):
        split_by_mask(forward_masked, lo, count, block, first_row)

    def fwd_both(block, carry):
        forward_block(0, rows, block, early_first)
        return carry

    def fwd_late(block, carry):
        forward_block(half, half, block, late_first)
        return carry

    lax.fori_loop(0, early_blocks, fwd_both, 0)
    lax.fori_loop(early_blocks, late_blocks, fwd_late, 0)

    attention = (acc_ref[...] / total_ref[...]).astype(jnp.bfloat16)
    out_ref[...] = attention
    lse_ref[...] = top_ref[...] + jnp.log(total_ref[...])
    dot_ref[...] = jnp.sum(
        g_ref[...].astype(jnp.float32) * attention.astype(jnp.float32), axis=1, keepdims=True
    )
    dqacc_ref[...] = jnp.zeros(dqacc_ref.shape, jnp.float32)
    dkv_ref[...] = jnp.zeros(dkv_ref.shape, jnp.float32)

    def backward_masked(lo, count, start, masked):
        s = scores_of(lo, count, start, masked)
        probs = jnp.exp(s - lse_ref[lo:lo + count, :])
        g = g_ref[lo:lo + count, :]
        k = kv_ref[pl.ds(start, KEY_BLOCK), 0:width]
        v = kv_ref[pl.ds(start, KEY_BLOCK), width:2 * width]
        grad_probs = lax.dot_general(g, v, (((1,), (1,)), ((), ())), preferred_element_type=jnp.float32)
        grad_scores = (probs * (grad_probs - dot_ref[lo:lo + count, :])).astype(jnp.bfloat16)
        dqacc_ref[lo:lo + count, :] += jnp.dot(grad_scores, k, preferred_element_type=jnp.float32)
        q = q_ref[lo:lo + count, :]
        dk = lax.dot_general(grad_scores, q, (((0,), (0,)), ((), ())), preferred_element_type=jnp.float32)
        dv = lax.dot_general(
            probs.astype(jnp.bfloat16), g, (((0,), (0,)), ((), ())), preferred_element_type=jnp.float32
        )
        dkv_ref[pl.ds(start, KEY_BLOCK), 0:width] += dk
        dkv_ref[pl.ds(start, KEY_BLOCK), width:2 * width] += dv

    def bwd_both(block, carry):
        split_by_mask(backward_masked, 0, rows, block, early_first)
        return carry

    def bwd_late(block, carry):
        split_by_mask(backward_masked, half, half, block, late_first)
        return carry

    lax.fori_loop(0, early_blocks, bwd_both, 0)
    lax.fori_loop(early_blocks, late_blocks, bwd_late, 0)
    dq_ref[...] = (dqacc_ref[...] * scale).astype(jnp.bfloat16)


def shifted(array, axis, by):
    length = lax.axis_size(axis)
    return lax.ppermute(array, axis, [(i, (i + by) % length) for i in range(length)])


def local_attention(limits, q_rows, g_rows, kv_sorted, q_pos):
    rows, width = q_rows.shape
    keys = kv_sorted.shape[0]
    vmem = pltpu.VMEM
    flops = 2 * rows * keys * width * 7 // 2
    return pl.pallas_call(
        attention_kernel,
        out_shape=(
            jax.ShapeDtypeStruct((rows, width), jnp.bfloat16),
            jax.ShapeDtypeStruct((rows, width), jnp.bfloat16),
            jax.ShapeDtypeStruct((keys, 2 * width), jnp.float32),
        ),
        in_specs=[
            pl.BlockSpec(memory_space=pltpu.SMEM),
            pl.BlockSpec(memory_space=vmem),
            pl.BlockSpec(memory_space=vmem),
            pl.BlockSpec(memory_space=vmem),
            pl.BlockSpec(memory_space=vmem),
        ],
        out_specs=(
            pl.BlockSpec(memory_space=vmem),
            pl.BlockSpec(memory_space=vmem),
            pl.BlockSpec(memory_space=vmem),
        ),
        scratch_shapes=[
            pltpu.VMEM((rows, 1), jnp.float32),
            pltpu.VMEM((rows, 1), jnp.float32),
            pltpu.VMEM((rows, width), jnp.float32),
            pltpu.VMEM((rows, 1), jnp.float32),
            pltpu.VMEM((rows, 1), jnp.float32),
            pltpu.VMEM((rows, width), jnp.float32),
        ],
        cost_estimate=pl.CostEstimate(
            flops=flops, transcendentals=rows * keys, bytes_accessed=keys * width * 12
        ),
    )(limits, q_rows, g_rows, kv_sorted, q_pos)


def on_device(queries, keys, values, out_grad, order):
    row_count = queries.shape[0]
    width = HEAD_DIM
    score_scale = 1.0 / math.sqrt(width)
    cycle_size = lax.axis_size(CTX)
    span_count = 2 * cycle_size
    my_index = lax.axis_index(CTX)
    q_heads = queries.shape[1] // width

    outer = lax.axis_size("zh")
    inner = lax.axis_size("y")
    kv_local = jnp.concatenate([keys, values], axis=1)
    column = lax.all_gather(kv_local, "zh", axis=0, tiled=True)
    rightward = [column]
    leftward = [column]
    for _ in range(inner // 2):
        rightward.append(shifted(rightward[-1], "y", 1))
    for _ in range((inner - 1) // 2):
        leftward.append(shifted(leftward[-1], "y", -1))
    by_distance = leftward + rightward[1:][::-1]
    kv_all = jnp.concatenate(by_distance, axis=0)
    my_y = lax.axis_index("y")
    inverse = jnp.zeros((span_count,), jnp.int32).at[order].set(jnp.arange(span_count, dtype=jnp.int32))
    holder = inverse // 2
    distance = (holder % inner - my_y + inner) % inner
    gathered_at = 2 * (distance * outer + holder // inner) + inverse % 2
    kv_sorted = kv_all.reshape(span_count, SPAN, 2 * width)[gathered_at].reshape(span_count * SPAN, 2 * width)

    pair = lax.dynamic_slice_in_dim(order, 2 * my_index, 2)
    low_first = pair[0] < pair[1]
    my_low = jnp.minimum(pair[0], pair[1])
    early_keys = (my_low + 1) * SPAN
    late_keys = (span_count - my_low) * SPAN
    limits = jnp.stack(
        [
            (early_keys + KEY_BLOCK - 1) // KEY_BLOCK,
            (late_keys + KEY_BLOCK - 1) // KEY_BLOCK,
            my_low * SPAN,
            (span_count - 1 - my_low) * SPAN,
        ]
    ).astype(jnp.int32)

    def to_rows(array):
        blocks = array.reshape(2, SPAN, q_heads, width)
        blocks = jnp.where(low_first, blocks, blocks[::-1])
        return blocks.transpose(0, 2, 1, 3).reshape(2 * q_heads * SPAN, width)

    def from_rows(array):
        blocks = array.reshape(2, q_heads, SPAN, width).transpose(0, 2, 1, 3)
        blocks = jnp.where(low_first, blocks, blocks[::-1])
        return blocks.reshape(row_count, q_heads * width)

    offsets = jnp.arange(SPAN, dtype=jnp.int32)
    span_pos = jnp.stack([my_low, span_count - 1 - my_low])[:, None] * SPAN + offsets[None, :]
    q_pos = jnp.broadcast_to(span_pos[:, None, :], (2, q_heads, SPAN)).reshape(-1, 1)

    attention_rows, dq_rows, dkv_sorted = local_attention(
        limits, to_rows(queries), to_rows(out_grad), kv_sorted, q_pos
    )
    owner_zh = jnp.arange(outer, dtype=jnp.int32)[:, None, None]
    owner_y = (my_y + jnp.arange(inner, dtype=jnp.int32)[None, :, None]) % inner
    half_block = jnp.arange(2, dtype=jnp.int32)[None, None, :]
    by_owner = 2 * (owner_zh * inner + owner_y) + half_block
    dkv_all = dkv_sorted.reshape(span_count, SPAN, 2 * width)[order[by_owner]]
    dkv_all = dkv_all.reshape(outer, inner, 2 * SPAN, 2 * width)

    def part(step):
        return dkv_all[:, step % inner]

    right = part(inner // 2)
    for step in range(inner // 2 - 1, 0, -1):
        right = shifted(right.astype(jnp.bfloat16), "y", 1).astype(jnp.float32) + part(step)
    right = shifted(right.astype(jnp.bfloat16), "y", 1).astype(jnp.float32)
    left = part(inner // 2 + 1)
    for step in range(inner // 2 + 2, inner):
        left = shifted(left.astype(jnp.bfloat16), "y", -1).astype(jnp.float32) + part(step)
    left = shifted(left.astype(jnp.bfloat16), "y", -1).astype(jnp.float32)
    row_sums = right + left + part(0)
    dkv_parts = lax.all_to_all(row_sums.astype(jnp.bfloat16), "zh", 0, 0, tiled=False)
    dkv_mine = jnp.sum(dkv_parts.astype(jnp.float32), axis=0)
    grad_keys = (score_scale * dkv_mine[:, :width]).astype(jnp.bfloat16)
    grad_values = dkv_mine[:, width:].astype(jnp.bfloat16)
    return (from_rows(attention_rows), from_rows(dq_rows), grad_keys, grad_values)


def solution(mesh):
    ctx_size = mesh.shape["ctx"]
    outer = 4 if ctx_size % 4 == 0 else 1
    split = Mesh(
        mesh.devices.reshape(outer, ctx_size // outer, mesh.shape["head"]), ("zh", "y", "head")
    )
    rows = P(CTX, "head")
    return jax.shard_map(
        on_device,
        mesh=split,
        in_specs=(rows, rows, rows, rows, P()),
        out_specs=(rows, rows, rows, rows),
        check_vma=False,
    )
```

```python
import math

import jax
import jax.numpy as jnp
from jax import lax
from jax.experimental import pallas as pl
from jax.experimental.pallas import tpu as pltpu
from jax.sharding import Mesh
from jax.sharding import PartitionSpec as P

HEADS = 32
KV_HEADS = 8
HEAD_DIM = 128
SPAN = 80
KEY_BLOCK = 1024

NEG = -1e30
CTX = ("zh", "y")


def attention_kernel(
    limits_ref, source_ref, target_ref, q_ref, g_ref, kv_in_ref, qpos_ref,
    out_ref, dq_ref, dkv_out_ref,
    top_ref, total_ref, acc_ref, lse_ref, dot_ref, dqacc_ref, kv_ref, dkv_ref,
):
    rows = q_ref.shape[0]
    spans = source_ref.shape[0]

    def sort_span(span, carry):
        source = pl.multiple_of(source_ref[span] * SPAN, 16)
        kv_ref[pl.ds(pl.multiple_of(span * SPAN, 16), SPAN), :] = kv_in_ref[pl.ds(source, SPAN), :]
        return carry

    lax.fori_loop(0, spans, sort_span, 0)
    half = rows // 2
    width = HEAD_DIM
    scale = 1.0 / math.sqrt(width)
    early_blocks = limits_ref[0]
    late_blocks = limits_ref[1]
    early_first = limits_ref[2]
    late_first = limits_ref[3]

    top_ref[...] = jnp.full(top_ref.shape, NEG, jnp.float32)
    total_ref[...] = jnp.zeros(total_ref.shape, jnp.float32)
    acc_ref[...] = jnp.zeros(acc_ref.shape, jnp.float32)

    def scores_of(lo, count, start, masked):
        q = q_ref[lo:lo + count, :]
        k = kv_ref[pl.ds(start, KEY_BLOCK), 0:width]
        s = lax.dot_general(q, k, (((1,), (1,)), ((), ())), preferred_element_type=jnp.float32) * scale
        if masked:
            kpos = start + lax.broadcasted_iota(jnp.int32, (1, KEY_BLOCK), 1)
            s = jnp.where(kpos <= qpos_ref[lo:lo + count, :], s, NEG)
        return s

    def forward_masked(lo, count, start, masked):
        s = scores_of(lo, count, start, masked)
        old_top = top_ref[lo:lo + count, :]
        new_top = jnp.maximum(old_top, jnp.max(s, axis=1, keepdims=True))
        p = jnp.exp(s - new_top)
        rescale = jnp.exp(old_top - new_top)
        total_ref[lo:lo + count, :] = total_ref[lo:lo + count, :] * rescale + jnp.sum(p, axis=1, keepdims=True)
        v = kv_ref[pl.ds(start, KEY_BLOCK), width:2 * width]
        pv = jnp.dot(p.astype(jnp.bfloat16), v, preferred_element_type=jnp.float32)
        acc_ref[lo:lo + count, :] = acc_ref[lo:lo + count, :] * rescale + pv
        top_ref[lo:lo + count, :] = new_top

    def split_by_mask(body, lo, count, block, first_row):
        start = pl.multiple_of(block * KEY_BLOCK, KEY_BLOCK)
        needs_mask = start + KEY_BLOCK - 1 > first_row

        @pl.when(needs_mask)
        def _():
            body(lo, count, start, True)

        @pl.when(jnp.logical_not(needs_mask))
        def _():
            body(lo, count, start, False)

    def forward_block(lo, count, block, first_row):
        split_by_mask(forward_masked, lo, count, block, first_row)

    def fwd_both(block, carry):
        forward_block(0, rows, block, early_first)
        return carry

    def fwd_late(block, carry):
        forward_block(half, half, block, late_first)
        return carry

    lax.fori_loop(0, early_blocks, fwd_both, 0)
    lax.fori_loop(early_blocks, late_blocks, fwd_late, 0)

    attention = (acc_ref[...] / total_ref[...]).astype(jnp.bfloat16)
    out_ref[...] = attention
    lse_ref[...] = top_ref[...] + jnp.log(total_ref[...])
    dot_ref[...] = jnp.sum(
        g_ref[...].astype(jnp.float32) * attention.astype(jnp.float32), axis=1, keepdims=True
    )
    dqacc_ref[...] = jnp.zeros(dqacc_ref.shape, jnp.float32)
    dkv_ref[...] = jnp.zeros(dkv_ref.shape, jnp.float32)

    def backward_masked(lo, count, start, masked):
        s = scores_of(lo, count, start, masked)
        probs = jnp.exp(s - lse_ref[lo:lo + count, :])
        g = g_ref[lo:lo + count, :]
        k = kv_ref[pl.ds(start, KEY_BLOCK), 0:width]
        v = kv_ref[pl.ds(start, KEY_BLOCK), width:2 * width]
        grad_probs = lax.dot_general(g, v, (((1,), (1,)), ((), ())), preferred_element_type=jnp.float32)
        grad_scores = (probs * (grad_probs - dot_ref[lo:lo + count, :])).astype(jnp.bfloat16)
        dqacc_ref[lo:lo + count, :] += jnp.dot(grad_scores, k, preferred_element_type=jnp.float32)
        q = q_ref[lo:lo + count, :]
        dk = lax.dot_general(grad_scores, q, (((0,), (0,)), ((), ())), preferred_element_type=jnp.float32)
        dv = lax.dot_general(
            probs.astype(jnp.bfloat16), g, (((0,), (0,)), ((), ())), preferred_element_type=jnp.float32
        )
        dkv_ref[pl.ds(start, KEY_BLOCK), 0:width] += dk
        dkv_ref[pl.ds(start, KEY_BLOCK), width:2 * width] += dv

    def bwd_both(block, carry):
        split_by_mask(backward_masked, 0, rows, block, early_first)
        return carry

    def bwd_late(block, carry):
        split_by_mask(backward_masked, half, half, block, late_first)
        return carry

    lax.fori_loop(0, early_blocks, bwd_both, 0)
    lax.fori_loop(early_blocks, late_blocks, bwd_late, 0)
    dq_ref[...] = (dqacc_ref[...] * scale).astype(jnp.bfloat16)

    def place_span(span, carry):
        target = pl.multiple_of(target_ref[span] * SPAN, 16)
        block = dkv_ref[pl.ds(pl.multiple_of(span * SPAN, 16), SPAN), :]
        dkv_out_ref[pl.ds(target, SPAN), :] = block.astype(jnp.bfloat16)
        return carry

    lax.fori_loop(0, spans, place_span, 0)


def shifted(array, axis, by):
    length = lax.axis_size(axis)
    return lax.ppermute(array, axis, [(i, (i + by) % length) for i in range(length)])


def local_attention(limits, source, target, q_rows, g_rows, kv_gathered, q_pos):
    rows, width = q_rows.shape
    keys = kv_gathered.shape[0]
    vmem = pltpu.VMEM
    flops = 2 * rows * keys * width * 7 // 2
    return pl.pallas_call(
        attention_kernel,
        out_shape=(
            jax.ShapeDtypeStruct((rows, width), jnp.bfloat16),
            jax.ShapeDtypeStruct((rows, width), jnp.bfloat16),
            jax.ShapeDtypeStruct((keys, 2 * width), jnp.bfloat16),
        ),
        in_specs=[
            pl.BlockSpec(memory_space=pltpu.SMEM),
            pl.BlockSpec(memory_space=pltpu.SMEM),
            pl.BlockSpec(memory_space=pltpu.SMEM),
            pl.BlockSpec(memory_space=vmem),
            pl.BlockSpec(memory_space=vmem),
            pl.BlockSpec(memory_space=vmem),
            pl.BlockSpec(memory_space=vmem),
        ],
        out_specs=(
            pl.BlockSpec(memory_space=vmem),
            pl.BlockSpec(memory_space=vmem),
            pl.BlockSpec(memory_space=vmem),
        ),
        scratch_shapes=[
            pltpu.VMEM((rows, 1), jnp.float32),
            pltpu.VMEM((rows, 1), jnp.float32),
            pltpu.VMEM((rows, width), jnp.float32),
            pltpu.VMEM((rows, 1), jnp.float32),
            pltpu.VMEM((rows, 1), jnp.float32),
            pltpu.VMEM((rows, width), jnp.float32),
            pltpu.VMEM((keys, 2 * width), jnp.bfloat16),
            pltpu.VMEM((keys, 2 * width), jnp.float32),
        ],
        cost_estimate=pl.CostEstimate(
            flops=flops, transcendentals=rows * keys, bytes_accessed=keys * width * 12
        ),
    )(limits, source, target, q_rows, g_rows, kv_gathered, q_pos)


def on_device(queries, keys, values, out_grad, order):
    row_count = queries.shape[0]
    width = HEAD_DIM
    score_scale = 1.0 / math.sqrt(width)
    cycle_size = lax.axis_size(CTX)
    span_count = 2 * cycle_size
    my_index = lax.axis_index(CTX)
    q_heads = queries.shape[1] // width

    outer = lax.axis_size("zh")
    inner = lax.axis_size("y")
    kv_local = jnp.concatenate([keys, values], axis=1)
    column = lax.all_gather(kv_local, "zh", axis=0, tiled=True)
    rightward = [column]
    leftward = [column]
    for _ in range(inner // 2):
        rightward.append(shifted(rightward[-1], "y", 1))
    for _ in range((inner - 1) // 2):
        leftward.append(shifted(leftward[-1], "y", -1))
    by_distance = leftward + rightward[1:][::-1]
    kv_all = jnp.concatenate(by_distance, axis=0)
    my_y = lax.axis_index("y")
    inverse = jnp.zeros((span_count,), jnp.int32).at[order].set(jnp.arange(span_count, dtype=jnp.int32))
    holder = inverse // 2
    distance = (holder % inner - my_y + inner) % inner
    gathered_at = 2 * (distance * outer + holder // inner) + inverse % 2

    pair = lax.dynamic_slice_in_dim(order, 2 * my_index, 2)
    low_first = pair[0] < pair[1]
    my_low = jnp.minimum(pair[0], pair[1])
    early_keys = (my_low + 1) * SPAN
    late_keys = (span_count - my_low) * SPAN
    limits = jnp.stack(
        [
            (early_keys + KEY_BLOCK - 1) // KEY_BLOCK,
            (late_keys + KEY_BLOCK - 1) // KEY_BLOCK,
            my_low * SPAN,
            (span_count - 1 - my_low) * SPAN,
        ]
    ).astype(jnp.int32)

    def to_rows(array):
        blocks = array.reshape(2, SPAN, q_heads, width)
        blocks = jnp.where(low_first, blocks, blocks[::-1])
        return blocks.transpose(0, 2, 1, 3).reshape(2 * q_heads * SPAN, width)

    def from_rows(array):
        blocks = array.reshape(2, q_heads, SPAN, width).transpose(0, 2, 1, 3)
        blocks = jnp.where(low_first, blocks, blocks[::-1])
        return blocks.reshape(row_count, q_heads * width)

    offsets = jnp.arange(SPAN, dtype=jnp.int32)
    span_pos = jnp.stack([my_low, span_count - 1 - my_low])[:, None] * SPAN + offsets[None, :]
    q_pos = jnp.broadcast_to(span_pos[:, None, :], (2, q_heads, SPAN)).reshape(-1, 1)

    attention_rows, dq_rows, dkv_placed = local_attention(
        limits, gathered_at, inverse, to_rows(queries), to_rows(out_grad), kv_all, q_pos
    )
    dkv_all = dkv_placed.reshape(outer, inner, 2 * SPAN, 2 * width)
    row_parts = lax.all_to_all(dkv_all, "y", 1, 1, tiled=False)
    row_sums = jnp.sum(row_parts.astype(jnp.float32), axis=1)
    dkv_parts = lax.all_to_all(row_sums.astype(jnp.bfloat16), "zh", 0, 0, tiled=False)
    dkv_mine = jnp.sum(dkv_parts.astype(jnp.float32), axis=0)
    grad_keys = (score_scale * dkv_mine[:, :width]).astype(jnp.bfloat16)
    grad_values = dkv_mine[:, width:].astype(jnp.bfloat16)
    return (from_rows(attention_rows), from_rows(dq_rows), grad_keys, grad_values)


def solution(mesh):
    ctx_size = mesh.shape["ctx"]
    outer = 4 if ctx_size % 4 == 0 else 1
    split = Mesh(
        mesh.devices.reshape(outer, ctx_size // outer, mesh.shape["head"]), ("zh", "y", "head")
    )
    rows = P(CTX, "head")
    return jax.shard_map(
        on_device,
        mesh=split,
        in_specs=(rows, rows, rows, rows, P()),
        out_specs=(rows, rows, rows, rows),
        check_vma=False,
    )
```

```python
import math

import jax
import jax.numpy as jnp
from jax import lax
from jax.experimental import pallas as pl
from jax.experimental.pallas import tpu as pltpu
from jax.sharding import Mesh
from jax.sharding import PartitionSpec as P

HEADS = 32
KV_HEADS = 8
HEAD_DIM = 128
SPAN = 80
KEY_BLOCK = 1024

NEG = -1e30
CTX = ("zh", "y")


def attention_kernel(
    limits_ref, source_ref, target_ref, q_ref, g_ref, kv_in_ref, qpos_ref,
    out_ref, dq_ref, dkv_out_ref,
    top_ref, total_ref, acc_ref, lse_ref, dot_ref, dqacc_ref, kv_ref, dkv_ref,
):
    rows = q_ref.shape[0]
    spans = source_ref.shape[0]

    def sort_span(span, carry):
        source = pl.multiple_of(source_ref[span] * SPAN, 16)
        kv_ref[pl.ds(pl.multiple_of(span * SPAN, 16), SPAN), :] = kv_in_ref[pl.ds(source, SPAN), :]
        return carry

    lax.fori_loop(0, spans, sort_span, 0)
    half = rows // 2
    width = HEAD_DIM
    scale = 1.0 / math.sqrt(width)
    early_blocks = limits_ref[0]
    late_blocks = limits_ref[1]
    early_first = limits_ref[2]
    late_first = limits_ref[3]

    top_ref[...] = jnp.full(top_ref.shape, NEG, jnp.float32)
    total_ref[...] = jnp.zeros(total_ref.shape, jnp.float32)
    acc_ref[...] = jnp.zeros(acc_ref.shape, jnp.float32)

    def scores_of(lo, count, start, masked):
        q = q_ref[lo:lo + count, :]
        k = kv_ref[pl.ds(start, KEY_BLOCK), 0:width]
        s = lax.dot_general(q, k, (((1,), (1,)), ((), ())), preferred_element_type=jnp.float32) * scale
        if masked:
            kpos = start + lax.broadcasted_iota(jnp.int32, (1, KEY_BLOCK), 1)
            s = jnp.where(kpos <= qpos_ref[lo:lo + count, :], s, NEG)
        return s

    def forward_masked(lo, count, start, masked):
        s = scores_of(lo, count, start, masked)
        old_top = top_ref[lo:lo + count, :]
        new_top = jnp.maximum(old_top, jnp.max(s, axis=1, keepdims=True))
        p = jnp.exp(s - new_top)
        rescale = jnp.exp(old_top - new_top)
        total_ref[lo:lo + count, :] = total_ref[lo:lo + count, :] * rescale + jnp.sum(p, axis=1, keepdims=True)
        v = kv_ref[pl.ds(start, KEY_BLOCK), width:2 * width]
        pv = jnp.dot(p.astype(jnp.bfloat16), v, preferred_element_type=jnp.float32)
        acc_ref[lo:lo + count, :] = acc_ref[lo:lo + count, :] * rescale + pv
        top_ref[lo:lo + count, :] = new_top

    def split_by_mask(body, lo, count, block, first_row):
        start = pl.multiple_of(block * KEY_BLOCK, KEY_BLOCK)
        needs_mask = start + KEY_BLOCK - 1 > first_row

        @pl.when(needs_mask)
        def _():
            body(lo, count, start, True)

        @pl.when(jnp.logical_not(needs_mask))
        def _():
            body(lo, count, start, False)

    def forward_block(lo, count, block, first_row):
        split_by_mask(forward_masked, lo, count, block, first_row)

    def fwd_both(block, carry):
        forward_block(0, rows, block, early_first)
        return carry

    def fwd_late(block, carry):
        forward_block(half, half, block, late_first)
        return carry

    lax.fori_loop(0, early_blocks, fwd_both, 0)
    lax.fori_loop(early_blocks, late_blocks, fwd_late, 0)

    attention = (acc_ref[...] / total_ref[...]).astype(jnp.bfloat16)
    out_ref[...] = attention
    lse_ref[...] = top_ref[...] + jnp.log(total_ref[...])
    dot_ref[...] = jnp.sum(
        g_ref[...].astype(jnp.float32) * attention.astype(jnp.float32), axis=1, keepdims=True
    )
    dqacc_ref[...] = jnp.zeros(dqacc_ref.shape, jnp.float32)
    dkv_ref[...] = jnp.zeros(dkv_ref.shape, jnp.float32)

    def backward_masked(lo, count, start, masked):
        s = scores_of(lo, count, start, masked)
        probs = jnp.exp(s - lse_ref[lo:lo + count, :])
        g = g_ref[lo:lo + count, :]
        k = kv_ref[pl.ds(start, KEY_BLOCK), 0:width]
        v = kv_ref[pl.ds(start, KEY_BLOCK), width:2 * width]
        grad_probs = lax.dot_general(g, v, (((1,), (1,)), ((), ())), preferred_element_type=jnp.float32)
        grad_scores = (probs * (grad_probs - dot_ref[lo:lo + count, :])).astype(jnp.bfloat16)
        dqacc_ref[lo:lo + count, :] += jnp.dot(grad_scores, k, preferred_element_type=jnp.float32)
        q = q_ref[lo:lo + count, :]
        dk = lax.dot_general(grad_scores, q, (((0,), (0,)), ((), ())), preferred_element_type=jnp.float32)
        dv = lax.dot_general(
            probs.astype(jnp.bfloat16), g, (((0,), (0,)), ((), ())), preferred_element_type=jnp.float32
        )
        dkv_ref[pl.ds(start, KEY_BLOCK), 0:width] += dk
        dkv_ref[pl.ds(start, KEY_BLOCK), width:2 * width] += dv

    def bwd_both(block, carry):
        split_by_mask(backward_masked, 0, rows, block, early_first)
        return carry

    def bwd_late(block, carry):
        split_by_mask(backward_masked, half, half, block, late_first)
        return carry

    lax.fori_loop(0, early_blocks, bwd_both, 0)
    lax.fori_loop(early_blocks, late_blocks, bwd_late, 0)
    dq_ref[...] = (dqacc_ref[...] * scale).astype(jnp.bfloat16)

    def place_span(span, carry):
        target = pl.multiple_of(target_ref[span] * SPAN, 16)
        block = dkv_ref[pl.ds(pl.multiple_of(span * SPAN, 16), SPAN), :]
        dkv_out_ref[pl.ds(target, SPAN), :] = block.astype(jnp.bfloat16)
        return carry

    lax.fori_loop(0, spans, place_span, 0)


def shifted(array, axis, by):
    length = lax.axis_size(axis)
    return lax.ppermute(array, axis, [(i, (i + by) % length) for i in range(length)])


def local_attention(limits, source, target, q_rows, g_rows, kv_gathered, q_pos):
    rows, width = q_rows.shape
    keys = kv_gathered.shape[0]
    vmem = pltpu.VMEM
    flops = 2 * rows * keys * width * 7 // 2
    return pl.pallas_call(
        attention_kernel,
        out_shape=(
            jax.ShapeDtypeStruct((rows, width), jnp.bfloat16),
            jax.ShapeDtypeStruct((rows, width), jnp.bfloat16),
            jax.ShapeDtypeStruct((keys, 2 * width), jnp.bfloat16),
        ),
        in_specs=[
            pl.BlockSpec(memory_space=pltpu.SMEM),
            pl.BlockSpec(memory_space=pltpu.SMEM),
            pl.BlockSpec(memory_space=pltpu.SMEM),
            pl.BlockSpec(memory_space=vmem),
            pl.BlockSpec(memory_space=vmem),
            pl.BlockSpec(memory_space=vmem),
            pl.BlockSpec(memory_space=vmem),
        ],
        out_specs=(
            pl.BlockSpec(memory_space=vmem),
            pl.BlockSpec(memory_space=vmem),
            pl.BlockSpec(memory_space=vmem),
        ),
        scratch_shapes=[
            pltpu.VMEM((rows, 1), jnp.float32),
            pltpu.VMEM((rows, 1), jnp.float32),
            pltpu.VMEM((rows, width), jnp.float32),
            pltpu.VMEM((rows, 1), jnp.float32),
            pltpu.VMEM((rows, 1), jnp.float32),
            pltpu.VMEM((rows, width), jnp.float32),
            pltpu.VMEM((keys, 2 * width), jnp.bfloat16),
            pltpu.VMEM((keys, 2 * width), jnp.float32),
        ],
        cost_estimate=pl.CostEstimate(
            flops=flops, transcendentals=rows * keys, bytes_accessed=keys * width * 12
        ),
    )(limits, source, target, q_rows, g_rows, kv_gathered, q_pos)


def on_device(queries, keys, values, out_grad, order):
    row_count = queries.shape[0]
    width = HEAD_DIM
    score_scale = 1.0 / math.sqrt(width)
    cycle_size = lax.axis_size(CTX)
    span_count = 2 * cycle_size
    my_index = lax.axis_index(CTX)
    q_heads = queries.shape[1] // width

    outer = lax.axis_size("zh")
    inner = lax.axis_size("y")
    kv_local = jnp.concatenate([keys, values], axis=1)
    column = lax.all_gather(kv_local, "zh", axis=0, tiled=True)
    rightward = [column]
    leftward = [column]
    for _ in range(inner // 2):
        rightward.append(shifted(rightward[-1], "y", 1))
    for _ in range((inner - 1) // 2):
        leftward.append(shifted(leftward[-1], "y", -1))
    by_distance = leftward + rightward[1:][::-1]
    kv_all = jnp.concatenate(by_distance, axis=0)
    my_y = lax.axis_index("y")
    inverse = jnp.zeros((span_count,), jnp.int32).at[order].set(jnp.arange(span_count, dtype=jnp.int32))
    holder = inverse // 2
    distance = (holder % inner - my_y + inner) % inner
    gathered_at = 2 * (distance * outer + holder // inner) + inverse % 2
    placed_at = 2 * ((holder % inner) * outer + holder // inner) + inverse % 2

    pair = lax.dynamic_slice_in_dim(order, 2 * my_index, 2)
    low_first = pair[0] < pair[1]
    my_low = jnp.minimum(pair[0], pair[1])
    early_keys = (my_low + 1) * SPAN
    late_keys = (span_count - my_low) * SPAN
    limits = jnp.stack(
        [
            (early_keys + KEY_BLOCK - 1) // KEY_BLOCK,
            (late_keys + KEY_BLOCK - 1) // KEY_BLOCK,
            my_low * SPAN,
            (span_count - 1 - my_low) * SPAN,
        ]
    ).astype(jnp.int32)

    def to_rows(array):
        blocks = array.reshape(2, SPAN, q_heads, width)
        blocks = jnp.where(low_first, blocks, blocks[::-1])
        return blocks.transpose(0, 2, 1, 3).reshape(2 * q_heads * SPAN, width)

    def from_rows(array):
        blocks = array.reshape(2, q_heads, SPAN, width).transpose(0, 2, 1, 3)
        blocks = jnp.where(low_first, blocks, blocks[::-1])
        return blocks.reshape(row_count, q_heads * width)

    offsets = jnp.arange(SPAN, dtype=jnp.int32)
    span_pos = jnp.stack([my_low, span_count - 1 - my_low])[:, None] * SPAN + offsets[None, :]
    q_pos = jnp.broadcast_to(span_pos[:, None, :], (2, q_heads, SPAN)).reshape(-1, 1)

    attention_rows, dq_rows, dkv_placed = local_attention(
        limits, gathered_at, placed_at, to_rows(queries), to_rows(out_grad), kv_all, q_pos
    )
    dkv_all = dkv_placed.reshape(inner, outer, 2 * SPAN, 2 * width)
    row_parts = lax.all_to_all(dkv_all, "y", 0, 0, tiled=False)
    row_sums = jnp.sum(row_parts.astype(jnp.float32), axis=0)
    dkv_parts = lax.all_to_all(row_sums.astype(jnp.bfloat16), "zh", 0, 0, tiled=False)
    dkv_mine = jnp.sum(dkv_parts.astype(jnp.float32), axis=0)
    grad_keys = (score_scale * dkv_mine[:, :width]).astype(jnp.bfloat16)
    grad_values = dkv_mine[:, width:].astype(jnp.bfloat16)
    return (from_rows(attention_rows), from_rows(dq_rows), grad_keys, grad_values)


def solution(mesh):
    ctx_size = mesh.shape["ctx"]
    outer = 4 if ctx_size % 4 == 0 else 1
    split = Mesh(
        mesh.devices.reshape(outer, ctx_size // outer, mesh.shape["head"]), ("zh", "y", "head")
    )
    rows = P(CTX, "head")
    return jax.shard_map(
        on_device,
        mesh=split,
        in_specs=(rows, rows, rows, rows, P()),
        out_specs=(rows, rows, rows, rows),
        check_vma=False,
    )
```

```python
import math

import jax
import jax.numpy as jnp
from jax import lax
from jax.experimental import pallas as pl
from jax.experimental.pallas import tpu as pltpu
from jax.sharding import Mesh
from jax.sharding import PartitionSpec as P

HEADS = 32
KV_HEADS = 8
HEAD_DIM = 128
SPAN = 80
KEY_BLOCK = 1024

NEG = -1e30
CTX = ("zh", "y")


def attention_kernel(
    limits_ref, source_ref, target_ref, q_ref, g_ref, kv_in_ref, qpos_ref,
    out_ref, dq_ref, dkv_out_ref,
    top_ref, total_ref, acc_ref, lse_ref, dot_ref, dqacc_ref, kv_ref, dkv_ref,
):
    rows = q_ref.shape[0]
    spans = source_ref.shape[0]

    def sort_span(span, carry):
        source = pl.multiple_of(source_ref[span] * SPAN, 16)
        kv_ref[pl.ds(pl.multiple_of(span * SPAN, 16), SPAN), :] = kv_in_ref[pl.ds(source, SPAN), :]
        return carry

    lax.fori_loop(0, spans, sort_span, 0)
    half = rows // 2
    width = HEAD_DIM
    scale = 1.0 / math.sqrt(width)
    early_blocks = limits_ref[0]
    late_blocks = limits_ref[1]
    early_first = limits_ref[2]
    late_first = limits_ref[3]

    top_ref[...] = jnp.full(top_ref.shape, NEG, jnp.float32)
    total_ref[...] = jnp.zeros(total_ref.shape, jnp.float32)
    acc_ref[...] = jnp.zeros(acc_ref.shape, jnp.float32)

    def scores_of(lo, count, start, masked):
        q = q_ref[lo:lo + count, :]
        k = kv_ref[pl.ds(start, KEY_BLOCK), 0:width]
        s = lax.dot_general(q, k, (((1,), (1,)), ((), ())), preferred_element_type=jnp.float32) * scale
        if masked:
            kpos = start + lax.broadcasted_iota(jnp.int32, (1, KEY_BLOCK), 1)
            s = jnp.where(kpos <= qpos_ref[lo:lo + count, :], s, NEG)
        return s

    def forward_masked(lo, count, start, masked):
        s = scores_of(lo, count, start, masked)
        old_top = top_ref[lo:lo + count, :]
        new_top = jnp.maximum(old_top, jnp.max(s, axis=1, keepdims=True))
        p = jnp.exp(s - new_top)
        rescale = jnp.exp(old_top - new_top)
        total_ref[lo:lo + count, :] = total_ref[lo:lo + count, :] * rescale + jnp.sum(p, axis=1, keepdims=True)
        v = kv_ref[pl.ds(start, KEY_BLOCK), width:2 * width]
        pv = jnp.dot(p.astype(jnp.bfloat16), v, preferred_element_type=jnp.float32)
        acc_ref[lo:lo + count, :] = acc_ref[lo:lo + count, :] * rescale + pv
        top_ref[lo:lo + count, :] = new_top

    def split_by_mask(body, lo, count, block, first_row):
        start = pl.multiple_of(block * KEY_BLOCK, KEY_BLOCK)
        needs_mask = start + KEY_BLOCK - 1 > first_row

        @pl.when(needs_mask)
        def _():
            body(lo, count, start, True)

        @pl.when(jnp.logical_not(needs_mask))
        def _():
            body(lo, count, start, False)

    def forward_block(lo, count, block, first_row):
        split_by_mask(forward_masked, lo, count, block, first_row)

    def fwd_both(block, carry):
        forward_block(0, rows, block, early_first)
        return carry

    def fwd_late(block, carry):
        forward_block(half, half, block, late_first)
        return carry

    lax.fori_loop(0, early_blocks, fwd_both, 0)
    lax.fori_loop(early_blocks, late_blocks, fwd_late, 0)

    attention = (acc_ref[...] / total_ref[...]).astype(jnp.bfloat16)
    out_ref[...] = attention
    lse_ref[...] = top_ref[...] + jnp.log(total_ref[...])
    dot_ref[...] = jnp.sum(
        g_ref[...].astype(jnp.float32) * attention.astype(jnp.float32), axis=1, keepdims=True
    )
    dqacc_ref[...] = jnp.zeros(dqacc_ref.shape, jnp.float32)
    dkv_ref[...] = jnp.zeros(dkv_ref.shape, jnp.float32)

    def backward_masked(lo, count, start, masked):
        s = scores_of(lo, count, start, masked)
        probs = jnp.exp(s - lse_ref[lo:lo + count, :])
        g = g_ref[lo:lo + count, :]
        k = kv_ref[pl.ds(start, KEY_BLOCK), 0:width]
        v = kv_ref[pl.ds(start, KEY_BLOCK), width:2 * width]
        grad_probs = lax.dot_general(g, v, (((1,), (1,)), ((), ())), preferred_element_type=jnp.float32)
        grad_scores = (probs * (grad_probs - dot_ref[lo:lo + count, :])).astype(jnp.bfloat16)
        dqacc_ref[lo:lo + count, :] += jnp.dot(grad_scores, k, preferred_element_type=jnp.float32)
        q = q_ref[lo:lo + count, :]
        dk = lax.dot_general(grad_scores, q, (((0,), (0,)), ((), ())), preferred_element_type=jnp.float32)
        dv = lax.dot_general(
            probs.astype(jnp.bfloat16), g, (((0,), (0,)), ((), ())), preferred_element_type=jnp.float32
        )
        dkv_ref[pl.ds(start, KEY_BLOCK), 0:width] += dk
        dkv_ref[pl.ds(start, KEY_BLOCK), width:2 * width] += dv

    def bwd_both(block, carry):
        split_by_mask(backward_masked, 0, rows, block, early_first)
        return carry

    def bwd_late(block, carry):
        split_by_mask(backward_masked, half, half, block, late_first)
        return carry

    lax.fori_loop(0, early_blocks, bwd_both, 0)
    lax.fori_loop(early_blocks, late_blocks, bwd_late, 0)
    dq_ref[...] = (dqacc_ref[...] * scale).astype(jnp.bfloat16)

    def place_span(span, carry):
        target = pl.multiple_of(target_ref[span] * SPAN, 16)
        block = dkv_ref[pl.ds(pl.multiple_of(span * SPAN, 16), SPAN), :]
        dkv_out_ref[pl.ds(target, SPAN), :] = block.astype(jnp.bfloat16)
        return carry

    lax.fori_loop(0, spans, place_span, 0)


def shifted(array, axis, by):
    length = lax.axis_size(axis)
    return lax.ppermute(array, axis, [(i, (i + by) % length) for i in range(length)])


def local_attention(limits, source, target, q_rows, g_rows, kv_gathered, q_pos):
    rows, width = q_rows.shape
    keys = kv_gathered.shape[0]
    vmem = pltpu.VMEM
    flops = 2 * rows * keys * width * 7 // 2
    return pl.pallas_call(
        attention_kernel,
        out_shape=(
            jax.ShapeDtypeStruct((rows, width), jnp.bfloat16),
            jax.ShapeDtypeStruct((rows, width), jnp.bfloat16),
            jax.ShapeDtypeStruct((keys, 2 * width), jnp.bfloat16),
        ),
        in_specs=[
            pl.BlockSpec(memory_space=pltpu.SMEM),
            pl.BlockSpec(memory_space=pltpu.SMEM),
            pl.BlockSpec(memory_space=pltpu.SMEM),
            pl.BlockSpec(memory_space=vmem),
            pl.BlockSpec(memory_space=vmem),
            pl.BlockSpec(memory_space=vmem),
            pl.BlockSpec(memory_space=vmem),
        ],
        out_specs=(
            pl.BlockSpec(memory_space=vmem),
            pl.BlockSpec(memory_space=vmem),
            pl.BlockSpec(memory_space=vmem),
        ),
        scratch_shapes=[
            pltpu.VMEM((rows, 1), jnp.float32),
            pltpu.VMEM((rows, 1), jnp.float32),
            pltpu.VMEM((rows, width), jnp.float32),
            pltpu.VMEM((rows, 1), jnp.float32),
            pltpu.VMEM((rows, 1), jnp.float32),
            pltpu.VMEM((rows, width), jnp.float32),
            pltpu.VMEM((keys, 2 * width), jnp.bfloat16),
            pltpu.VMEM((keys, 2 * width), jnp.float32),
        ],
        cost_estimate=pl.CostEstimate(
            flops=flops, transcendentals=rows * keys, bytes_accessed=keys * width * 12
        ),
    )(limits, source, target, q_rows, g_rows, kv_gathered, q_pos)


def on_device(queries, keys, values, out_grad, order):
    row_count = queries.shape[0]
    width = HEAD_DIM
    score_scale = 1.0 / math.sqrt(width)
    cycle_size = lax.axis_size(CTX)
    span_count = 2 * cycle_size
    my_index = lax.axis_index(CTX)
    q_heads = queries.shape[1] // width

    outer = lax.axis_size("zh")
    inner = lax.axis_size("y")
    kv_local = jnp.concatenate([keys, values], axis=1)
    copies = jnp.broadcast_to(kv_local[None], (outer,) + kv_local.shape)
    column = lax.all_to_all(copies, "zh", 0, 0, tiled=False).reshape(outer * 2 * SPAN, 2 * width)
    rightward = [column]
    leftward = [column]
    for _ in range(inner // 2):
        rightward.append(shifted(rightward[-1], "y", 1))
    for _ in range((inner - 1) // 2):
        leftward.append(shifted(leftward[-1], "y", -1))
    by_distance = leftward + rightward[1:][::-1]
    kv_all = jnp.concatenate(by_distance, axis=0)
    my_y = lax.axis_index("y")
    inverse = jnp.zeros((span_count,), jnp.int32).at[order].set(jnp.arange(span_count, dtype=jnp.int32))
    holder = inverse // 2
    distance = (holder % inner - my_y + inner) % inner
    gathered_at = 2 * (distance * outer + holder // inner) + inverse % 2
    placed_at = 2 * ((holder % inner) * outer + holder // inner) + inverse % 2

    pair = lax.dynamic_slice_in_dim(order, 2 * my_index, 2)
    low_first = pair[0] < pair[1]
    my_low = jnp.minimum(pair[0], pair[1])
    early_keys = (my_low + 1) * SPAN
    late_keys = (span_count - my_low) * SPAN
    limits = jnp.stack(
        [
            (early_keys + KEY_BLOCK - 1) // KEY_BLOCK,
            (late_keys + KEY_BLOCK - 1) // KEY_BLOCK,
            my_low * SPAN,
            (span_count - 1 - my_low) * SPAN,
        ]
    ).astype(jnp.int32)

    def to_rows(array):
        blocks = array.reshape(2, SPAN, q_heads, width)
        blocks = jnp.where(low_first, blocks, blocks[::-1])
        return blocks.transpose(0, 2, 1, 3).reshape(2 * q_heads * SPAN, width)

    def from_rows(array):
        blocks = array.reshape(2, q_heads, SPAN, width).transpose(0, 2, 1, 3)
        blocks = jnp.where(low_first, blocks, blocks[::-1])
        return blocks.reshape(row_count, q_heads * width)

    offsets = jnp.arange(SPAN, dtype=jnp.int32)
    span_pos = jnp.stack([my_low, span_count - 1 - my_low])[:, None] * SPAN + offsets[None, :]
    q_pos = jnp.broadcast_to(span_pos[:, None, :], (2, q_heads, SPAN)).reshape(-1, 1)

    attention_rows, dq_rows, dkv_placed = local_attention(
        limits, gathered_at, placed_at, to_rows(queries), to_rows(out_grad), kv_all, q_pos
    )
    dkv_all = dkv_placed.reshape(inner, outer, 2 * SPAN, 2 * width)
    row_parts = lax.all_to_all(dkv_all, "y", 0, 0, tiled=False)
    row_sums = jnp.sum(row_parts.astype(jnp.float32), axis=0)
    dkv_parts = lax.all_to_all(row_sums.astype(jnp.bfloat16), "zh", 0, 0, tiled=False)
    dkv_mine = jnp.sum(dkv_parts.astype(jnp.float32), axis=0)
    grad_keys = (score_scale * dkv_mine[:, :width]).astype(jnp.bfloat16)
    grad_values = dkv_mine[:, width:].astype(jnp.bfloat16)
    return (from_rows(attention_rows), from_rows(dq_rows), grad_keys, grad_values)


def solution(mesh):
    ctx_size = mesh.shape["ctx"]
    outer = 4 if ctx_size % 4 == 0 else 1
    split = Mesh(
        mesh.devices.reshape(outer, ctx_size // outer, mesh.shape["head"]), ("zh", "y", "head")
    )
    rows = P(CTX, "head")
    return jax.shard_map(
        on_device,
        mesh=split,
        in_specs=(rows, rows, rows, rows, P()),
        out_specs=(rows, rows, rows, rows),
        check_vma=False,
    )
```

```python
import math

import jax
import jax.numpy as jnp
from jax import lax
from jax.experimental import pallas as pl
from jax.experimental.pallas import tpu as pltpu
from jax.sharding import Mesh
from jax.sharding import PartitionSpec as P

HEADS = 32
KV_HEADS = 8
HEAD_DIM = 128
SPAN = 80
KEY_BLOCK = 1024

NEG = -1e30
CTX = ("zh", "y")


def attention_kernel(
    limits_ref, source_ref, target_ref, q_ref, g_ref, kv_in_ref, qpos_ref,
    out_ref, dq_ref, dkv_out_ref,
    top_ref, total_ref, acc_ref, lse_ref, dot_ref, dqacc_ref, kv_ref, dkv_ref,
):
    rows = q_ref.shape[0]
    spans = source_ref.shape[0]

    def sort_span(span, carry):
        source = pl.multiple_of(source_ref[span] * SPAN, 16)
        kv_ref[pl.ds(pl.multiple_of(span * SPAN, 16), SPAN), :] = kv_in_ref[pl.ds(source, SPAN), :]
        return carry

    lax.fori_loop(0, spans, sort_span, 0)
    half = rows // 2
    width = HEAD_DIM
    scale = 1.0 / math.sqrt(width)
    early_blocks = limits_ref[0]
    late_blocks = limits_ref[1]
    early_first = limits_ref[2]
    late_first = limits_ref[3]

    top_ref[...] = jnp.full(top_ref.shape, NEG, jnp.float32)
    total_ref[...] = jnp.zeros(total_ref.shape, jnp.float32)
    acc_ref[...] = jnp.zeros(acc_ref.shape, jnp.float32)

    def scores_of(lo, count, start, masked):
        q = q_ref[lo:lo + count, :]
        k = kv_ref[pl.ds(start, KEY_BLOCK), 0:width]
        s = lax.dot_general(q, k, (((1,), (1,)), ((), ())), preferred_element_type=jnp.float32) * scale
        if masked:
            kpos = start + lax.broadcasted_iota(jnp.int32, (1, KEY_BLOCK), 1)
            s = jnp.where(kpos <= qpos_ref[lo:lo + count, :], s, NEG)
        return s

    def forward_masked(lo, count, start, masked):
        s = scores_of(lo, count, start, masked)
        old_top = top_ref[lo:lo + count, :]
        new_top = jnp.maximum(old_top, jnp.max(s, axis=1, keepdims=True))
        p = jnp.exp(s - new_top)
        rescale = jnp.exp(old_top - new_top)
        total_ref[lo:lo + count, :] = total_ref[lo:lo + count, :] * rescale + jnp.sum(p, axis=1, keepdims=True)
        v = kv_ref[pl.ds(start, KEY_BLOCK), width:2 * width]
        pv = jnp.dot(p.astype(jnp.bfloat16), v, preferred_element_type=jnp.float32)
        acc_ref[lo:lo + count, :] = acc_ref[lo:lo + count, :] * rescale + pv
        top_ref[lo:lo + count, :] = new_top

    def split_by_mask(body, lo, count, block, first_row):
        start = pl.multiple_of(block * KEY_BLOCK, KEY_BLOCK)
        needs_mask = start + KEY_BLOCK - 1 > first_row

        @pl.when(needs_mask)
        def _():
            body(lo, count, start, True)

        @pl.when(jnp.logical_not(needs_mask))
        def _():
            body(lo, count, start, False)

    def forward_block(lo, count, block, first_row):
        split_by_mask(forward_masked, lo, count, block, first_row)

    def fwd_both(block, carry):
        forward_block(0, rows, block, early_first)
        return carry

    def fwd_late(block, carry):
        forward_block(half, half, block, late_first)
        return carry

    lax.fori_loop(0, early_blocks, fwd_both, 0)
    lax.fori_loop(early_blocks, late_blocks, fwd_late, 0)

    attention = (acc_ref[...] / total_ref[...]).astype(jnp.bfloat16)
    out_ref[...] = attention
    lse_ref[...] = top_ref[...] + jnp.log(total_ref[...])
    dot_ref[...] = jnp.sum(
        g_ref[...].astype(jnp.float32) * attention.astype(jnp.float32), axis=1, keepdims=True
    )
    dqacc_ref[...] = jnp.zeros(dqacc_ref.shape, jnp.float32)

    def clear_block(block, carry):
        start = pl.multiple_of(block * KEY_BLOCK, KEY_BLOCK)
        dkv_ref[pl.ds(start, KEY_BLOCK), :] = jnp.zeros((KEY_BLOCK, dkv_ref.shape[1]), jnp.float32)
        return carry

    lax.fori_loop(late_blocks, dkv_ref.shape[0] // KEY_BLOCK, clear_block, 0)

    def backward_masked(lo, count, start, masked):
        s = scores_of(lo, count, start, masked)
        probs = jnp.exp(s - lse_ref[lo:lo + count, :])
        g = g_ref[lo:lo + count, :]
        k = kv_ref[pl.ds(start, KEY_BLOCK), 0:width]
        v = kv_ref[pl.ds(start, KEY_BLOCK), width:2 * width]
        grad_probs = lax.dot_general(g, v, (((1,), (1,)), ((), ())), preferred_element_type=jnp.float32)
        grad_scores = (probs * (grad_probs - dot_ref[lo:lo + count, :])).astype(jnp.bfloat16)
        dqacc_ref[lo:lo + count, :] += jnp.dot(grad_scores, k, preferred_element_type=jnp.float32)
        q = q_ref[lo:lo + count, :]
        dk = lax.dot_general(grad_scores, q, (((0,), (0,)), ((), ())), preferred_element_type=jnp.float32)
        dv = lax.dot_general(
            probs.astype(jnp.bfloat16), g, (((0,), (0,)), ((), ())), preferred_element_type=jnp.float32
        )
        dkv_ref[pl.ds(start, KEY_BLOCK), 0:width] = dk
        dkv_ref[pl.ds(start, KEY_BLOCK), width:2 * width] = dv

    def bwd_both(block, carry):
        split_by_mask(backward_masked, 0, rows, block, early_first)
        return carry

    def bwd_late(block, carry):
        split_by_mask(backward_masked, half, half, block, late_first)
        return carry

    lax.fori_loop(0, early_blocks, bwd_both, 0)
    lax.fori_loop(early_blocks, late_blocks, bwd_late, 0)
    dq_ref[...] = (dqacc_ref[...] * scale).astype(jnp.bfloat16)

    def place_span(span, carry):
        target = pl.multiple_of(target_ref[span] * SPAN, 16)
        block = dkv_ref[pl.ds(pl.multiple_of(span * SPAN, 16), SPAN), :]
        dkv_out_ref[pl.ds(target, SPAN), :] = block.astype(jnp.bfloat16)
        return carry

    lax.fori_loop(0, spans, place_span, 0)


def shifted(array, axis, by):
    length = lax.axis_size(axis)
    return lax.ppermute(array, axis, [(i, (i + by) % length) for i in range(length)])


def local_attention(limits, source, target, q_rows, g_rows, kv_gathered, q_pos):
    rows, width = q_rows.shape
    keys = kv_gathered.shape[0]
    vmem = pltpu.VMEM
    flops = 2 * rows * keys * width * 7 // 2
    return pl.pallas_call(
        attention_kernel,
        out_shape=(
            jax.ShapeDtypeStruct((rows, width), jnp.bfloat16),
            jax.ShapeDtypeStruct((rows, width), jnp.bfloat16),
            jax.ShapeDtypeStruct((keys, 2 * width), jnp.bfloat16),
        ),
        in_specs=[
            pl.BlockSpec(memory_space=pltpu.SMEM),
            pl.BlockSpec(memory_space=pltpu.SMEM),
            pl.BlockSpec(memory_space=pltpu.SMEM),
            pl.BlockSpec(memory_space=vmem),
            pl.BlockSpec(memory_space=vmem),
            pl.BlockSpec(memory_space=vmem),
            pl.BlockSpec(memory_space=vmem),
        ],
        out_specs=(
            pl.BlockSpec(memory_space=vmem),
            pl.BlockSpec(memory_space=vmem),
            pl.BlockSpec(memory_space=vmem),
        ),
        scratch_shapes=[
            pltpu.VMEM((rows, 1), jnp.float32),
            pltpu.VMEM((rows, 1), jnp.float32),
            pltpu.VMEM((rows, width), jnp.float32),
            pltpu.VMEM((rows, 1), jnp.float32),
            pltpu.VMEM((rows, 1), jnp.float32),
            pltpu.VMEM((rows, width), jnp.float32),
            pltpu.VMEM((keys, 2 * width), jnp.bfloat16),
            pltpu.VMEM((keys, 2 * width), jnp.float32),
        ],
        cost_estimate=pl.CostEstimate(
            flops=flops, transcendentals=rows * keys, bytes_accessed=keys * width * 12
        ),
    )(limits, source, target, q_rows, g_rows, kv_gathered, q_pos)


def on_device(queries, keys, values, out_grad, order):
    row_count = queries.shape[0]
    width = HEAD_DIM
    score_scale = 1.0 / math.sqrt(width)
    cycle_size = lax.axis_size(CTX)
    span_count = 2 * cycle_size
    my_index = lax.axis_index(CTX)
    q_heads = queries.shape[1] // width

    outer = lax.axis_size("zh")
    inner = lax.axis_size("y")
    kv_local = jnp.concatenate([keys, values], axis=1)
    column = lax.all_gather(kv_local, "zh", axis=0, tiled=True)
    rightward = [column]
    leftward = [column]
    for _ in range(inner // 2):
        rightward.append(shifted(rightward[-1], "y", 1))
    for _ in range((inner - 1) // 2):
        leftward.append(shifted(leftward[-1], "y", -1))
    by_distance = leftward + rightward[1:][::-1]
    kv_all = jnp.concatenate(by_distance, axis=0)
    my_y = lax.axis_index("y")
    inverse = jnp.zeros((span_count,), jnp.int32).at[order].set(jnp.arange(span_count, dtype=jnp.int32))
    holder = inverse // 2
    distance = (holder % inner - my_y + inner) % inner
    gathered_at = 2 * (distance * outer + holder // inner) + inverse % 2
    placed_at = 2 * ((holder % inner) * outer + holder // inner) + inverse % 2

    pair = lax.dynamic_slice_in_dim(order, 2 * my_index, 2)
    low_first = pair[0] < pair[1]
    my_low = jnp.minimum(pair[0], pair[1])
    early_keys = (my_low + 1) * SPAN
    late_keys = (span_count - my_low) * SPAN
    limits = jnp.stack(
        [
            (early_keys + KEY_BLOCK - 1) // KEY_BLOCK,
            (late_keys + KEY_BLOCK - 1) // KEY_BLOCK,
            my_low * SPAN,
            (span_count - 1 - my_low) * SPAN,
        ]
    ).astype(jnp.int32)

    def to_rows(array):
        blocks = array.reshape(2, SPAN, q_heads, width)
        blocks = jnp.where(low_first, blocks, blocks[::-1])
        return blocks.transpose(0, 2, 1, 3).reshape(2 * q_heads * SPAN, width)

    def from_rows(array):
        blocks = array.reshape(2, q_heads, SPAN, width).transpose(0, 2, 1, 3)
        blocks = jnp.where(low_first, blocks, blocks[::-1])
        return blocks.reshape(row_count, q_heads * width)

    offsets = jnp.arange(SPAN, dtype=jnp.int32)
    span_pos = jnp.stack([my_low, span_count - 1 - my_low])[:, None] * SPAN + offsets[None, :]
    q_pos = jnp.broadcast_to(span_pos[:, None, :], (2, q_heads, SPAN)).reshape(-1, 1)

    attention_rows, dq_rows, dkv_placed = local_attention(
        limits, gathered_at, placed_at, to_rows(queries), to_rows(out_grad), kv_all, q_pos
    )
    dkv_all = dkv_placed.reshape(inner, outer, 2 * SPAN, 2 * width)
    row_parts = lax.all_to_all(dkv_all, "y", 0, 0, tiled=False)
    row_sums = jnp.sum(row_parts.astype(jnp.float32), axis=0)
    dkv_parts = lax.all_to_all(row_sums.astype(jnp.bfloat16), "zh", 0, 0, tiled=False)
    dkv_mine = jnp.sum(dkv_parts.astype(jnp.float32), axis=0)
    grad_keys = (score_scale * dkv_mine[:, :width]).astype(jnp.bfloat16)
    grad_values = dkv_mine[:, width:].astype(jnp.bfloat16)
    return (from_rows(attention_rows), from_rows(dq_rows), grad_keys, grad_values)


def solution(mesh):
    ctx_size = mesh.shape["ctx"]
    outer = 4 if ctx_size % 4 == 0 else 1
    split = Mesh(
        mesh.devices.reshape(outer, ctx_size // outer, mesh.shape["head"]), ("zh", "y", "head")
    )
    rows = P(CTX, "head")
    return jax.shard_map(
        on_device,
        mesh=split,
        in_specs=(rows, rows, rows, rows, P()),
        out_specs=(rows, rows, rows, rows),
        check_vma=False,
    )
```

```python
import math

import jax
import jax.numpy as jnp
from jax import lax
from jax.experimental import pallas as pl
from jax.experimental.pallas import tpu as pltpu
from jax.sharding import Mesh
from jax.sharding import PartitionSpec as P

HEADS = 32
KV_HEADS = 8
HEAD_DIM = 128
SPAN = 80
KEY_BLOCK = 1024

NEG = -1e30
CTX = ("zh", "y")


def attention_kernel(
    limits_ref, source_ref, target_ref, q_ref, g_ref, kv_in_ref, qpos_ref,
    out_ref, dq_ref, dkv_out_ref,
    top_ref, total_ref, acc_ref, lse_ref, dot_ref, dqacc_ref, kv_ref, dkv_ref,
):
    rows = q_ref.shape[0]
    spans = source_ref.shape[0]

    def sort_span(span, carry):
        source = pl.multiple_of(source_ref[span] * SPAN, 16)
        kv_ref[pl.ds(pl.multiple_of(span * SPAN, 16), SPAN), :] = kv_in_ref[pl.ds(source, SPAN), :]
        return carry

    lax.fori_loop(0, spans, sort_span, 0)
    half = rows // 2
    width = HEAD_DIM
    scale = 1.0 / math.sqrt(width)
    early_blocks = limits_ref[0]
    late_blocks = limits_ref[1]
    early_first = limits_ref[2]
    late_first = limits_ref[3]

    top_ref[...] = jnp.full(top_ref.shape, NEG, jnp.float32)
    total_ref[...] = jnp.zeros(total_ref.shape, jnp.float32)
    acc_ref[...] = jnp.zeros(acc_ref.shape, jnp.float32)

    def scores_of(lo, count, start, masked):
        q = q_ref[lo:lo + count, :]
        k = kv_ref[pl.ds(start, KEY_BLOCK), 0:width]
        s = lax.dot_general(q, k, (((1,), (1,)), ((), ())), preferred_element_type=jnp.float32) * scale
        if masked:
            kpos = start + lax.broadcasted_iota(jnp.int32, (1, KEY_BLOCK), 1)
            s = jnp.where(kpos <= qpos_ref[lo:lo + count, :], s, NEG)
        return s

    def forward_masked(lo, count, start, masked):
        s = scores_of(lo, count, start, masked)
        old_top = top_ref[lo:lo + count, :]
        new_top = jnp.maximum(old_top, jnp.max(s, axis=1, keepdims=True))
        p = jnp.exp(s - new_top)
        rescale = jnp.exp(old_top - new_top)
        total_ref[lo:lo + count, :] = total_ref[lo:lo + count, :] * rescale + jnp.sum(p, axis=1, keepdims=True)
        v = kv_ref[pl.ds(start, KEY_BLOCK), width:2 * width]
        pv = jnp.dot(p.astype(jnp.bfloat16), v, preferred_element_type=jnp.float32)
        acc_ref[lo:lo + count, :] = acc_ref[lo:lo + count, :] * rescale + pv
        top_ref[lo:lo + count, :] = new_top

    def split_by_mask(body, lo, count, block, first_row):
        start = pl.multiple_of(block * KEY_BLOCK, KEY_BLOCK)
        needs_mask = start + KEY_BLOCK - 1 > first_row

        @pl.when(needs_mask)
        def _():
            body(lo, count, start, True)

        @pl.when(jnp.logical_not(needs_mask))
        def _():
            body(lo, count, start, False)

    def forward_block(lo, count, block, first_row):
        split_by_mask(forward_masked, lo, count, block, first_row)

    def fwd_both(block, carry):
        forward_block(0, rows, block, early_first)
        return carry

    def fwd_late(block, carry):
        forward_block(half, half, block, late_first)
        return carry

    lax.fori_loop(0, early_blocks, fwd_both, 0)
    lax.fori_loop(early_blocks, late_blocks, fwd_late, 0)

    attention = (acc_ref[...] / total_ref[...]).astype(jnp.bfloat16)
    out_ref[...] = attention
    lse_ref[...] = top_ref[...] + jnp.log(total_ref[...])
    dot_ref[...] = jnp.sum(
        g_ref[...].astype(jnp.float32) * attention.astype(jnp.float32), axis=1, keepdims=True
    )
    dqacc_ref[...] = jnp.zeros(dqacc_ref.shape, jnp.float32)

    def clear_block(block, carry):
        start = pl.multiple_of(block * KEY_BLOCK, KEY_BLOCK)
        dkv_ref[pl.ds(start, KEY_BLOCK), :] = jnp.zeros((KEY_BLOCK, dkv_ref.shape[1]), jnp.bfloat16)
        return carry

    lax.fori_loop(late_blocks, dkv_ref.shape[0] // KEY_BLOCK, clear_block, 0)

    def backward_masked(lo, count, start, masked):
        s = scores_of(lo, count, start, masked)
        probs = jnp.exp(s - lse_ref[lo:lo + count, :])
        g = g_ref[lo:lo + count, :]
        k = kv_ref[pl.ds(start, KEY_BLOCK), 0:width]
        v = kv_ref[pl.ds(start, KEY_BLOCK), width:2 * width]
        grad_probs = lax.dot_general(g, v, (((1,), (1,)), ((), ())), preferred_element_type=jnp.float32)
        grad_scores = (probs * (grad_probs - dot_ref[lo:lo + count, :])).astype(jnp.bfloat16)
        dqacc_ref[lo:lo + count, :] += jnp.dot(grad_scores, k, preferred_element_type=jnp.float32)
        q = q_ref[lo:lo + count, :]
        dk = lax.dot_general(grad_scores, q, (((0,), (0,)), ((), ())), preferred_element_type=jnp.float32)
        dv = lax.dot_general(
            probs.astype(jnp.bfloat16), g, (((0,), (0,)), ((), ())), preferred_element_type=jnp.float32
        )
        dkv_ref[pl.ds(start, KEY_BLOCK), 0:width] = dk.astype(jnp.bfloat16)
        dkv_ref[pl.ds(start, KEY_BLOCK), width:2 * width] = dv.astype(jnp.bfloat16)

    def bwd_both(block, carry):
        split_by_mask(backward_masked, 0, rows, block, early_first)
        return carry

    def bwd_late(block, carry):
        split_by_mask(backward_masked, half, half, block, late_first)
        return carry

    lax.fori_loop(0, early_blocks, bwd_both, 0)
    lax.fori_loop(early_blocks, late_blocks, bwd_late, 0)
    dq_ref[...] = (dqacc_ref[...] * scale).astype(jnp.bfloat16)

    def place_span(span, carry):
        target = pl.multiple_of(target_ref[span] * SPAN, 16)
        block = dkv_ref[pl.ds(pl.multiple_of(span * SPAN, 16), SPAN), :]
        dkv_out_ref[pl.ds(target, SPAN), :] = block
        return carry

    lax.fori_loop(0, spans, place_span, 0)


def shifted(array, axis, by):
    length = lax.axis_size(axis)
    return lax.ppermute(array, axis, [(i, (i + by) % length) for i in range(length)])


def local_attention(limits, source, target, q_rows, g_rows, kv_gathered, q_pos):
    rows, width = q_rows.shape
    keys = kv_gathered.shape[0]
    vmem = pltpu.VMEM
    flops = 2 * rows * keys * width * 7 // 2
    return pl.pallas_call(
        attention_kernel,
        out_shape=(
            jax.ShapeDtypeStruct((rows, width), jnp.bfloat16),
            jax.ShapeDtypeStruct((rows, width), jnp.bfloat16),
            jax.ShapeDtypeStruct((keys, 2 * width), jnp.bfloat16),
        ),
        in_specs=[
            pl.BlockSpec(memory_space=pltpu.SMEM),
            pl.BlockSpec(memory_space=pltpu.SMEM),
            pl.BlockSpec(memory_space=pltpu.SMEM),
            pl.BlockSpec(memory_space=vmem),
            pl.BlockSpec(memory_space=vmem),
            pl.BlockSpec(memory_space=vmem),
            pl.BlockSpec(memory_space=vmem),
        ],
        out_specs=(
            pl.BlockSpec(memory_space=vmem),
            pl.BlockSpec(memory_space=vmem),
            pl.BlockSpec(memory_space=vmem),
        ),
        scratch_shapes=[
            pltpu.VMEM((rows, 1), jnp.float32),
            pltpu.VMEM((rows, 1), jnp.float32),
            pltpu.VMEM((rows, width), jnp.float32),
            pltpu.VMEM((rows, 1), jnp.float32),
            pltpu.VMEM((rows, 1), jnp.float32),
            pltpu.VMEM((rows, width), jnp.float32),
            pltpu.VMEM((keys, 2 * width), jnp.bfloat16),
            pltpu.VMEM((keys, 2 * width), jnp.bfloat16),
        ],
        cost_estimate=pl.CostEstimate(
            flops=flops, transcendentals=rows * keys, bytes_accessed=keys * width * 12
        ),
    )(limits, source, target, q_rows, g_rows, kv_gathered, q_pos)


def on_device(queries, keys, values, out_grad, order):
    row_count = queries.shape[0]
    width = HEAD_DIM
    score_scale = 1.0 / math.sqrt(width)
    cycle_size = lax.axis_size(CTX)
    span_count = 2 * cycle_size
    my_index = lax.axis_index(CTX)
    q_heads = queries.shape[1] // width

    outer = lax.axis_size("zh")
    inner = lax.axis_size("y")
    kv_local = jnp.concatenate([keys, values], axis=1)
    column = lax.all_gather(kv_local, "zh", axis=0, tiled=True)
    rightward = [column]
    leftward = [column]
    for _ in range(inner // 2):
        rightward.append(shifted(rightward[-1], "y", 1))
    for _ in range((inner - 1) // 2):
        leftward.append(shifted(leftward[-1], "y", -1))
    by_distance = leftward + rightward[1:][::-1]
    kv_all = jnp.concatenate(by_distance, axis=0)
    my_y = lax.axis_index("y")
    inverse = jnp.zeros((span_count,), jnp.int32).at[order].set(jnp.arange(span_count, dtype=jnp.int32))
    holder = inverse // 2
    distance = (holder % inner - my_y + inner) % inner
    gathered_at = 2 * (distance * outer + holder // inner) + inverse % 2
    placed_at = 2 * ((holder % inner) * outer + holder // inner) + inverse % 2

    pair = lax.dynamic_slice_in_dim(order, 2 * my_index, 2)
    low_first = pair[0] < pair[1]
    my_low = jnp.minimum(pair[0], pair[1])
    early_keys = (my_low + 1) * SPAN
    late_keys = (span_count - my_low) * SPAN
    limits = jnp.stack(
        [
            (early_keys + KEY_BLOCK - 1) // KEY_BLOCK,
            (late_keys + KEY_BLOCK - 1) // KEY_BLOCK,
            my_low * SPAN,
            (span_count - 1 - my_low) * SPAN,
        ]
    ).astype(jnp.int32)

    def to_rows(array):
        blocks = array.reshape(2, SPAN, q_heads, width)
        blocks = jnp.where(low_first, blocks, blocks[::-1])
        return blocks.transpose(0, 2, 1, 3).reshape(2 * q_heads * SPAN, width)

    def from_rows(array):
        blocks = array.reshape(2, q_heads, SPAN, width).transpose(0, 2, 1, 3)
        blocks = jnp.where(low_first, blocks, blocks[::-1])
        return blocks.reshape(row_count, q_heads * width)

    offsets = jnp.arange(SPAN, dtype=jnp.int32)
    span_pos = jnp.stack([my_low, span_count - 1 - my_low])[:, None] * SPAN + offsets[None, :]
    q_pos = jnp.broadcast_to(span_pos[:, None, :], (2, q_heads, SPAN)).reshape(-1, 1)

    attention_rows, dq_rows, dkv_placed = local_attention(
        limits, gathered_at, placed_at, to_rows(queries), to_rows(out_grad), kv_all, q_pos
    )
    dkv_all = dkv_placed.reshape(inner, outer, 2 * SPAN, 2 * width)
    row_parts = lax.all_to_all(dkv_all, "y", 0, 0, tiled=False)
    row_sums = jnp.sum(row_parts.astype(jnp.float32), axis=0)
    dkv_parts = lax.all_to_all(row_sums.astype(jnp.bfloat16), "zh", 0, 0, tiled=False)
    dkv_mine = jnp.sum(dkv_parts.astype(jnp.float32), axis=0)
    grad_keys = (score_scale * dkv_mine[:, :width]).astype(jnp.bfloat16)
    grad_values = dkv_mine[:, width:].astype(jnp.bfloat16)
    return (from_rows(attention_rows), from_rows(dq_rows), grad_keys, grad_values)


def solution(mesh):
    ctx_size = mesh.shape["ctx"]
    outer = 4 if ctx_size % 4 == 0 else 1
    split = Mesh(
        mesh.devices.reshape(outer, ctx_size // outer, mesh.shape["head"]), ("zh", "y", "head")
    )
    rows = P(CTX, "head")
    return jax.shard_map(
        on_device,
        mesh=split,
        in_specs=(rows, rows, rows, rows, P()),
        out_specs=(rows, rows, rows, rows),
        check_vma=False,
    )
```

```python
import math

import jax
import jax.numpy as jnp
from jax import lax
from jax.experimental import pallas as pl
from jax.experimental.pallas import tpu as pltpu
from jax.sharding import Mesh
from jax.sharding import PartitionSpec as P

HEADS = 32
KV_HEADS = 8
HEAD_DIM = 128
SPAN = 80
KEY_BLOCK = 1024

NEG = -1e30
CTX = ("zh", "y")


def attention_kernel(
    limits_ref, source_ref, target_ref, q_ref, g_ref, kv_in_ref, qpos_ref,
    out_ref, dq_ref, dkv_out_ref,
    top_ref, total_ref, acc_ref, lse_ref, dot_ref, dqacc_ref, kv_ref, dkv_ref,
):
    rows = q_ref.shape[0]
    spans = source_ref.shape[0]

    def sort_span(span, carry):
        source = pl.multiple_of(source_ref[span] * SPAN, 16)
        kv_ref[pl.ds(pl.multiple_of(span * SPAN, 16), SPAN), :] = kv_in_ref[pl.ds(source, SPAN), :]
        return carry

    lax.fori_loop(0, spans, sort_span, 0)
    half = rows // 2
    width = HEAD_DIM
    scale = 1.0 / math.sqrt(width)
    early_blocks = limits_ref[0]
    late_blocks = limits_ref[1]
    early_first = limits_ref[2]
    late_first = limits_ref[3]

    top_ref[...] = jnp.full(top_ref.shape, NEG, jnp.float32)
    total_ref[...] = jnp.zeros(total_ref.shape, jnp.float32)
    acc_ref[...] = jnp.zeros(acc_ref.shape, jnp.float32)

    def scores_of(lo, count, start, masked):
        q = q_ref[lo:lo + count, :]
        k = kv_ref[pl.ds(start, KEY_BLOCK), 0:width]
        s = lax.dot_general(q, k, (((1,), (1,)), ((), ())), preferred_element_type=jnp.float32) * scale
        if masked:
            kpos = start + lax.broadcasted_iota(jnp.int32, (1, KEY_BLOCK), 1)
            s = jnp.where(kpos <= qpos_ref[lo:lo + count, :], s, NEG)
        return s

    def forward_masked(lo, count, start, masked):
        s = scores_of(lo, count, start, masked)
        old_top = top_ref[lo:lo + count, :]
        new_top = jnp.maximum(old_top, jnp.max(s, axis=1, keepdims=True))
        p = jnp.exp(s - new_top)
        rescale = jnp.exp(old_top - new_top)
        total_ref[lo:lo + count, :] = total_ref[lo:lo + count, :] * rescale + jnp.sum(p, axis=1, keepdims=True)
        v = kv_ref[pl.ds(start, KEY_BLOCK), width:2 * width]
        pv = jnp.dot(p.astype(jnp.bfloat16), v, preferred_element_type=jnp.float32)
        acc_ref[lo:lo + count, :] = acc_ref[lo:lo + count, :] * rescale + pv
        top_ref[lo:lo + count, :] = new_top

    def split_by_mask(body, lo, count, block, first_row):
        start = pl.multiple_of(block * KEY_BLOCK, KEY_BLOCK)
        needs_mask = start + KEY_BLOCK - 1 > first_row

        @pl.when(needs_mask)
        def _():
            body(lo, count, start, True)

        @pl.when(jnp.logical_not(needs_mask))
        def _():
            body(lo, count, start, False)

    def forward_block(lo, count, block, first_row):
        split_by_mask(forward_masked, lo, count, block, first_row)

    def fwd_both(block, carry):
        forward_block(0, rows, block, early_first)
        return carry

    def fwd_late(block, carry):
        forward_block(half, half, block, late_first)
        return carry

    lax.fori_loop(0, early_blocks, fwd_both, 0)
    lax.fori_loop(early_blocks, late_blocks, fwd_late, 0)

    attention = (acc_ref[...] / total_ref[...]).astype(jnp.bfloat16)
    out_ref[...] = attention
    lse_ref[...] = top_ref[...] + jnp.log(total_ref[...])
    dot_ref[...] = jnp.sum(
        g_ref[...].astype(jnp.float32) * attention.astype(jnp.float32), axis=1, keepdims=True
    )

    def clear_block(block, carry):
        start = pl.multiple_of(block * KEY_BLOCK, KEY_BLOCK)
        dkv_ref[pl.ds(start, KEY_BLOCK), :] = jnp.zeros((KEY_BLOCK, dkv_ref.shape[1]), jnp.float32)
        return carry

    lax.fori_loop(late_blocks, dkv_ref.shape[0] // KEY_BLOCK, clear_block, 0)

    def backward_masked(lo, count, start, masked, first=False):
        s = scores_of(lo, count, start, masked)
        probs = jnp.exp(s - lse_ref[lo:lo + count, :])
        g = g_ref[lo:lo + count, :]
        k = kv_ref[pl.ds(start, KEY_BLOCK), 0:width]
        v = kv_ref[pl.ds(start, KEY_BLOCK), width:2 * width]
        grad_probs = lax.dot_general(g, v, (((1,), (1,)), ((), ())), preferred_element_type=jnp.float32)
        grad_scores = (probs * (grad_probs - dot_ref[lo:lo + count, :])).astype(jnp.bfloat16)
        dq_part = jnp.dot(grad_scores, k, preferred_element_type=jnp.float32)
        if first:
            dqacc_ref[lo:lo + count, :] = dq_part
        else:
            dqacc_ref[lo:lo + count, :] += dq_part
        q = q_ref[lo:lo + count, :]
        dk = lax.dot_general(grad_scores, q, (((0,), (0,)), ((), ())), preferred_element_type=jnp.float32)
        dv = lax.dot_general(
            probs.astype(jnp.bfloat16), g, (((0,), (0,)), ((), ())), preferred_element_type=jnp.float32
        )
        dkv_ref[pl.ds(start, KEY_BLOCK), 0:width] = dk
        dkv_ref[pl.ds(start, KEY_BLOCK), width:2 * width] = dv

    def bwd_both(block, carry):
        split_by_mask(backward_masked, 0, rows, block, early_first)
        return carry

    def bwd_late(block, carry):
        split_by_mask(backward_masked, half, half, block, late_first)
        return carry

    def backward_first(lo, count, start, masked):
        backward_masked(lo, count, start, masked, first=True)

    split_by_mask(backward_first, 0, rows, 0, early_first)
    lax.fori_loop(1, early_blocks, bwd_both, 0)
    lax.fori_loop(early_blocks, late_blocks, bwd_late, 0)
    dq_ref[...] = (dqacc_ref[...] * scale).astype(jnp.bfloat16)

    def place_span(span, carry):
        target = pl.multiple_of(target_ref[span] * SPAN, 16)
        block = dkv_ref[pl.ds(pl.multiple_of(span * SPAN, 16), SPAN), :]
        dkv_out_ref[pl.ds(target, SPAN), :] = block.astype(jnp.bfloat16)
        return carry

    lax.fori_loop(0, spans, place_span, 0)


def shifted(array, axis, by):
    length = lax.axis_size(axis)
    return lax.ppermute(array, axis, [(i, (i + by) % length) for i in range(length)])


def local_attention(limits, source, target, q_rows, g_rows, kv_gathered, q_pos):
    rows, width = q_rows.shape
    keys = kv_gathered.shape[0]
    vmem = pltpu.VMEM
    flops = 2 * rows * keys * width * 7 // 2
    return pl.pallas_call(
        attention_kernel,
        out_shape=(
            jax.ShapeDtypeStruct((rows, width), jnp.bfloat16),
            jax.ShapeDtypeStruct((rows, width), jnp.bfloat16),
            jax.ShapeDtypeStruct((keys, 2 * width), jnp.bfloat16),
        ),
        in_specs=[
            pl.BlockSpec(memory_space=pltpu.SMEM),
            pl.BlockSpec(memory_space=pltpu.SMEM),
            pl.BlockSpec(memory_space=pltpu.SMEM),
            pl.BlockSpec(memory_space=vmem),
            pl.BlockSpec(memory_space=vmem),
            pl.BlockSpec(memory_space=vmem),
            pl.BlockSpec(memory_space=vmem),
        ],
        out_specs=(
            pl.BlockSpec(memory_space=vmem),
            pl.BlockSpec(memory_space=vmem),
            pl.BlockSpec(memory_space=vmem),
        ),
        scratch_shapes=[
            pltpu.VMEM((rows, 1), jnp.float32),
            pltpu.VMEM((rows, 1), jnp.float32),
            pltpu.VMEM((rows, width), jnp.float32),
            pltpu.VMEM((rows, 1), jnp.float32),
            pltpu.VMEM((rows, 1), jnp.float32),
            pltpu.VMEM((rows, width), jnp.float32),
            pltpu.VMEM((keys, 2 * width), jnp.bfloat16),
            pltpu.VMEM((keys, 2 * width), jnp.float32),
        ],
        cost_estimate=pl.CostEstimate(
            flops=flops, transcendentals=rows * keys, bytes_accessed=keys * width * 12
        ),
    )(limits, source, target, q_rows, g_rows, kv_gathered, q_pos)


def on_device(queries, keys, values, out_grad, order):
    row_count = queries.shape[0]
    width = HEAD_DIM
    score_scale = 1.0 / math.sqrt(width)
    cycle_size = lax.axis_size(CTX)
    span_count = 2 * cycle_size
    my_index = lax.axis_index(CTX)
    q_heads = queries.shape[1] // width

    outer = lax.axis_size("zh")
    inner = lax.axis_size("y")
    kv_local = jnp.concatenate([keys, values], axis=1)
    column = lax.all_gather(kv_local, "zh", axis=0, tiled=True)
    rightward = [column]
    leftward = [column]
    for _ in range(inner // 2):
        rightward.append(shifted(rightward[-1], "y", 1))
    for _ in range((inner - 1) // 2):
        leftward.append(shifted(leftward[-1], "y", -1))
    by_distance = leftward + rightward[1:][::-1]
    kv_all = jnp.concatenate(by_distance, axis=0)
    my_y = lax.axis_index("y")
    inverse = jnp.zeros((span_count,), jnp.int32).at[order].set(jnp.arange(span_count, dtype=jnp.int32))
    holder = inverse // 2
    distance = (holder % inner - my_y + inner) % inner
    gathered_at = 2 * (distance * outer + holder // inner) + inverse % 2
    placed_at = 2 * ((holder % inner) * outer + holder // inner) + inverse % 2

    pair = lax.dynamic_slice_in_dim(order, 2 * my_index, 2)
    low_first = pair[0] < pair[1]
    my_low = jnp.minimum(pair[0], pair[1])
    early_keys = (my_low + 1) * SPAN
    late_keys = (span_count - my_low) * SPAN
    limits = jnp.stack(
        [
            (early_keys + KEY_BLOCK - 1) // KEY_BLOCK,
            (late_keys + KEY_BLOCK - 1) // KEY_BLOCK,
            my_low * SPAN,
            (span_count - 1 - my_low) * SPAN,
        ]
    ).astype(jnp.int32)

    def to_rows(array):
        blocks = array.reshape(2, SPAN, q_heads, width)
        blocks = jnp.where(low_first, blocks, blocks[::-1])
        return blocks.transpose(0, 2, 1, 3).reshape(2 * q_heads * SPAN, width)

    def from_rows(array):
        blocks = array.reshape(2, q_heads, SPAN, width).transpose(0, 2, 1, 3)
        blocks = jnp.where(low_first, blocks, blocks[::-1])
        return blocks.reshape(row_count, q_heads * width)

    offsets = jnp.arange(SPAN, dtype=jnp.int32)
    span_pos = jnp.stack([my_low, span_count - 1 - my_low])[:, None] * SPAN + offsets[None, :]
    q_pos = jnp.broadcast_to(span_pos[:, None, :], (2, q_heads, SPAN)).reshape(-1, 1)

    attention_rows, dq_rows, dkv_placed = local_attention(
        limits, gathered_at, placed_at, to_rows(queries), to_rows(out_grad), kv_all, q_pos
    )
    dkv_all = dkv_placed.reshape(inner, outer, 2 * SPAN, 2 * width)
    row_parts = lax.all_to_all(dkv_all, "y", 0, 0, tiled=False)
    row_sums = jnp.sum(row_parts.astype(jnp.float32), axis=0)
    dkv_parts = lax.all_to_all(row_sums.astype(jnp.bfloat16), "zh", 0, 0, tiled=False)
    dkv_mine = jnp.sum(dkv_parts.astype(jnp.float32), axis=0)
    grad_keys = (score_scale * dkv_mine[:, :width]).astype(jnp.bfloat16)
    grad_values = dkv_mine[:, width:].astype(jnp.bfloat16)
    return (from_rows(attention_rows), from_rows(dq_rows), grad_keys, grad_values)


def solution(mesh):
    ctx_size = mesh.shape["ctx"]
    outer = 4 if ctx_size % 4 == 0 else 1
    split = Mesh(
        mesh.devices.reshape(outer, ctx_size // outer, mesh.shape["head"]), ("zh", "y", "head")
    )
    rows = P(CTX, "head")
    return jax.shard_map(
        on_device,
        mesh=split,
        in_specs=(rows, rows, rows, rows, P()),
        out_specs=(rows, rows, rows, rows),
        check_vma=False,
    )
```
